256 devices in a mesh: ctx: 32 (over z, x_lo, core), head: 8 (over x_hi, y).
Axes of the slice: x: 4 (x_hi: 2, x_lo: 2; x = x_hi * 2 + x_lo), y: 4, z: 8, core: 2. Of those that a mesh axis runs over, the one named last changes fastest.
Arguments:
- queries: bfloat16 [8192, 24, 128], P('ctx', 'head'), may hold values from -4.5 to 4.5, as said below
- key_vectors: bfloat16 [8192, 24, 128], P('ctx', 'head'), may hold values from -4.5 to 4.5, as said below
- value_vectors: bfloat16 [8192, 24, 128], P('ctx', 'head'), may hold values from -6 to 6
- attn_output: bfloat16 [8192, 24, 128], P('ctx', 'head'), may hold values from -6 to 6
- output_grad: bfloat16 [8192, 5120], P('ctx', 'head'), may hold values from -6 to 6
- w_out: bfloat16 [3072, 5120], P('head'), may hold values from -0.078125 to 0.078125
- log_total: float32 [8192, 24], P('ctx', 'head'), as said below
Outputs:
- query_grad: bfloat16 [8192, 24, 128], P('ctx', 'head')
- key_grad: bfloat16 [8192, 24, 128], P('ctx', 'head')
- value_grad: bfloat16 [8192, 24, 128], P('ctx', 'head')
The draws below stay inside these ranges and needn't reach their ends.
Inputs may be any that keep to these rules, and one draw needn't show every extreme that they name: `queries`: independent entries of order one. `key_vectors`: entries of order one. `log_total`: for each position and head, the log of the sum of exp(scores) over the positions it sees, from the given queries and keys.
All inputs are finite; a program needn't handle non-finite values.
Results may differ from the reference program's by a relative error of at most 0.0058.
Values may be sent and summed in bfloat16 or wider, within the bound.
A program may use at most 128 MiB of HBM per device.

```python
import jax
import jax.numpy as jnp
from jax import lax

HEADS = 24
HEAD_DIM = 128
MODEL = 5120
TOKENS = 8192


def joint_draw(key):
    base_key = jax.random.fold_in(key, 101)
    full_shape = (TOKENS, HEADS, HEAD_DIM)
    query_draw = jax.random.normal(jax.random.fold_in(base_key, 1), full_shape, jnp.float32)
    key_draw = jax.random.normal(jax.random.fold_in(base_key, 2), full_shape, jnp.float32)
    query_draw = jnp.clip(query_draw, -4.5, 4.5)
    key_draw = jnp.clip(key_draw, -4.5, 4.5)
    query_round = query_draw.astype(jnp.bfloat16).astype(jnp.float32)
    key_round = key_draw.astype(jnp.bfloat16).astype(jnp.float32)
    position = jnp.arange(TOKENS, dtype=jnp.int32)
    causal = position[None, :] <= position[:, None]
    factor = HEAD_DIM ** (-0.5)

    def per_head(head_index):
        query_head = query_round[:, head_index, :]
        key_head = key_round[:, head_index, :]
        scores = jnp.dot(query_head, key_head.T, precision=lax.Precision.HIGHEST) * factor
        scores = jnp.where(causal, scores, -jnp.inf)
        return jax.nn.logsumexp(scores, axis=1)
    totals = lax.map(per_head, jnp.arange(HEADS, dtype=jnp.int32))
    return (query_draw, key_draw, jnp.transpose(totals, (1, 0)))


def draw_queries(key, part):
    return joint_draw(key)[0].astype(jnp.bfloat16)


def draw_key_vectors(key, part):
    return joint_draw(key)[1].astype(jnp.bfloat16)


def draw_log_total(key, part):
    return joint_draw(key)[2].astype(jnp.float32)


def steps_of(stream_key, shape, shards, smallest, largest):
    loudness, own = 1.0, jax.random.fold_in(stream_key, 6)
    for dim, shards_of in shards:
        heights = jnp.exp(jax.random.uniform(jax.random.fold_in(own, dim), (shards_of,), jnp.float32, smallest / len(shards), largest / len(shards)))
        loudness = loudness * jnp.repeat(heights, shape[dim] // shards_of).reshape([-1 if axis == dim else 1 for axis in range(len(shape))])
    return loudness


def scatter_about(own_key, dims, scale, reach, split=(), held_as=jnp.bfloat16):
    array = jax.random.normal(own_key, dims, jnp.float32) * scale
    if len(split) > 0:
        array = steps_of(own_key, dims, split, -0.22, 0.18) * array
    return jnp.clip(array, min=-reach, max=reach).astype(held_as)


def setup_inputs(seed: int = 0) -> dict:
    key_list = jax.random.split(jax.random.key(seed), 8)
    queries = draw_queries(jax.random.fold_in(key_list[7], 71), 0)
    key_vectors = draw_key_vectors(jax.random.fold_in(key_list[7], 71), 0)
    value_vectors = scatter_about(key_list[2], (TOKENS, HEADS, HEAD_DIM), 1.0, 6.0, ((0, 32), (1, 8)))
    attn_output = scatter_about(key_list[3], (TOKENS, HEADS, HEAD_DIM), 1.0, 6.0, ((0, 32), (1, 8)))
    output_grad = scatter_about(key_list[4], (TOKENS, MODEL), 1.0, 6.0, ((0, 32), (1, 8)))
    w_out = scatter_about(key_list[5], (HEADS * HEAD_DIM, MODEL), MODEL ** -0.5, 0.078125, ((0, 8),))
    log_total = draw_log_total(jax.random.fold_in(key_list[7], 71), 0)
    return {"queries": queries, "key_vectors": key_vectors, "value_vectors": value_vectors, "attn_output": attn_output, "output_grad": output_grad, "w_out": w_out, "log_total": log_total}


def reference(queries, key_vectors, value_vectors, attn_output, output_grad, w_out, log_total):
    factor = HEAD_DIM ** -0.5
    attn_grad = jnp.dot(output_grad, w_out.T, preferred_element_type=jnp.float32).astype(jnp.bfloat16)
    attn_grad = attn_grad.reshape(TOKENS, HEADS, HEAD_DIM)
    position = jnp.arange(TOKENS, dtype=jnp.int32)
    causal = position[None, :] <= position[:, None]

    def per_head(head_index):
        query_head = queries[:, head_index, :]
        key_head = key_vectors[:, head_index, :]
        value_head = value_vectors[:, head_index, :]
        output_head = attn_output[:, head_index, :]
        grad_head = attn_grad[:, head_index, :]
        total_head = log_total[:, head_index][:, None]
        raw_scores = jnp.dot(query_head, key_head.T, preferred_element_type=jnp.float32) * factor
        scores = jnp.where(causal, raw_scores, -jnp.inf)
        prob_full = jnp.exp(scores - total_head)
        prob_low = prob_full.astype(jnp.bfloat16)
        prob_grad = jnp.dot(grad_head, value_head.T, preferred_element_type=jnp.float32)
        row_delta = jnp.sum(grad_head.astype(jnp.float32) * output_head.astype(jnp.float32), axis=1, keepdims=True)
        score_grad = (prob_full * (prob_grad - row_delta)).astype(jnp.bfloat16)
        query_grad = (jnp.dot(score_grad, key_head, preferred_element_type=jnp.float32) * factor).astype(jnp.bfloat16)
        key_grad = (jnp.dot(score_grad.T, query_head, preferred_element_type=jnp.float32) * factor).astype(jnp.bfloat16)
        value_grad = jnp.dot(prob_low.T, grad_head, preferred_element_type=jnp.float32).astype(jnp.bfloat16)
        return query_grad, key_grad, value_grad

    query_grads, key_grads, value_grads = lax.map(per_head, jnp.arange(HEADS, dtype=jnp.int32))
    return (jnp.transpose(query_grads, (1, 0, 2)), jnp.transpose(key_grads, (1, 0, 2)), jnp.transpose(value_grads, (1, 0, 2)))
```

```python
import functools
import math

import jax
import jax.numpy as jnp
from jax import lax
from jax.experimental import pallas as pl
from jax.experimental.pallas import tpu as pltpu
from jax.sharding import PartitionSpec as P

MESH = pl.DeviceIdType.MESH
BF = jnp.bfloat16
F32 = jnp.float32
LOG2E = math.log2(math.e)
Z = 8
Y = 4

NT = (((1,), (1,)), ((), ()))
TN = (((0,), (0,)), ((), ()))
NN = (((1,), (0,)), ((), ()))


def mm(a, b, dims):
    return lax.dot_general(a, b, dims, preferred_element_type=F32)


def kernel(
    q_ref, k_ref, v_ref, o_ref, g_ref, lse_ref, w_hbm,
    dq_out, dk_out, dv_out,
    w_vm, gall, qall, kall, vall, doall, stat, dqb, sbuf, rbuf, rown,
    dkacc, dvacc, dq0, kv1s, kv1r, kv2s, kv2r,
    w_sem, send_sem, recv_sem,
):
    heads, rows, width = q_ref.shape
    half = rows // 2
    factor = width ** -0.5
    ctx = lax.axis_index("ctx")
    hd = lax.axis_index("head")
    z = ctx // 4
    p = ctx % 4
    xb, cb = p // 2, p % 2
    xh, y = hd // Y, hd % Y

    up = ((z + 1) % Z * 4 + p, hd)
    down = ((z + Z - 1) % Z * 4 + p, hd)
    north = (ctx, xh * Y + (y + 1) % Y)
    south = (ctx, xh * Y + (y + Y - 1) % Y)
    across = (ctx, (1 - xh) * Y + y)
    side = (z * 4 + (1 - xb) * 2 + cb, hd)
    twin = (z * 4 + xb * 2 + 1 - cb, hd)
    peers = (up, down, north, south, across, side, twin)

    counter = [0]

    def copy(src, dst, to):
        n = counter[0]
        counter[0] += 1
        return pltpu.make_async_remote_copy(
            src_ref=src, dst_ref=dst, send_sem=send_sem.at[n], recv_sem=recv_sem.at[n],
            device_id=to, device_id_type=MESH)

    wcopy = pltpu.make_async_copy(w_hbm, w_vm, w_sem)
    wcopy.start()

    barrier = pltpu.get_barrier_semaphore()
    for peer in peers:
        pl.semaphore_signal(barrier, inc=1, device_id=peer, device_id_type=MESH)
    pl.semaphore_wait(barrier, len(peers))

    started = []

    def go(src, dst, to):
        c = copy(src, dst, to)
        c.start()
        started.append(c)
        return c

    g01 = go(g_ref, gall.at[0, 1], south)
    g03 = go(g_ref, gall.at[0, 3], north)
    g10 = go(g_ref, gall.at[1, 0], across)
    q1 = go(q_ref, qall.at[1], down)
    q7 = go(q_ref, qall.at[7], up)
    k2 = go(k_ref, kall.at[:, 2], side)
    v2 = go(v_ref, vall.at[:, 2], side)
    k1 = go(k_ref, kall.at[:, 1], twin)
    v1 = go(v_ref, vall.at[:, 1], twin)

    qall[0] = q_ref[...]
    kall[:, 0] = k_ref[...]
    vall[:, 0] = v_ref[...]
    dqb[...] = jnp.zeros_like(dqb)
    dkacc[...] = jnp.zeros_like(dkacc)
    dvacc[...] = jnp.zeros_like(dvacc)
    wcopy.wait()

    def columns(a, b):
        at = ((xh + a) % 2 * Y + (y + b) % Y) * g_ref.shape[1]
        return pl.ds(pl.multiple_of(at, 128), g_ref.shape[1])

    def proj(a, b, block):
        return mm(block, w_vm[:, columns(a, b)], NT)

    acc = proj(0, 0, g_ref[...])

    q1.wait_recv()
    q2 = go(qall.at[1], qall.at[2], down)
    q7.wait_recv()
    q6 = go(qall.at[7], qall.at[6], up)
    g01.wait_recv()
    g02a = go(gall.at[0, 1, pl.ds(0, half)], gall.at[0, 2, pl.ds(0, half)], south)
    g03.wait_recv()
    g02b = go(gall.at[0, 3, pl.ds(half, half)], gall.at[0, 2, pl.ds(half, half)], north)
    acc += proj(0, 1, gall[0, 1])
    acc += proj(0, 3, gall[0, 3])
    q2.wait_recv()
    q3 = go(qall.at[2], qall.at[3], down)
    q6.wait_recv()
    q5 = go(qall.at[6], qall.at[5], up)
    g10.wait_recv()
    g11 = go(gall.at[1, 0], gall.at[1, 1], south)
    g13 = go(gall.at[1, 0], gall.at[1, 3], north)
    acc += proj(1, 0, gall[1, 0])
    k2.wait_recv()
    k3 = go(kall.at[:, 2], kall.at[:, 3], twin)
    v2.wait_recv()
    v3 = go(vall.at[:, 2], vall.at[:, 3], twin)
    q3.wait_recv()
    q4a = go(qall.at[3, :, pl.ds(0, half)], qall.at[4, :, pl.ds(0, half)], down)
    q5.wait_recv()
    q4b = go(qall.at[5, :, pl.ds(half, half)], qall.at[4, :, pl.ds(half, half)], up)
    g02a.wait_recv()
    g02b.wait_recv()
    acc += proj(0, 2, gall[0, 2])
    g11.wait_recv()
    g12a = go(gall.at[1, 1, pl.ds(0, half)], gall.at[1, 2, pl.ds(0, half)], south)
    g13.wait_recv()
    g12b = go(gall.at[1, 3, pl.ds(half, half)], gall.at[1, 2, pl.ds(half, half)], north)
    acc += proj(1, 1, gall[1, 1])
    acc += proj(1, 3, gall[1, 3])
    k1.wait_recv()
    v1.wait_recv()
    k3.wait_recv()
    v3.wait_recv()
    q4a.wait_recv()
    q4b.wait_recv()
    g12a.wait_recv()
    g12b.wait_recv()
    acc += proj(1, 2, gall[1, 2])

    grad = acc.astype(BF)
    stat[0] = jnp.zeros(stat.shape[1:], F32)
    for h in range(heads):
        grad_h = grad[:, h * width:(h + 1) * width]
        doall[0, h] = grad_h
        terms = grad_h.astype(F32) * o_ref[h].astype(F32)
        delta = jnp.sum(terms, axis=1, keepdims=True)
        stat[0, heads + h:heads + h + 1, :] = jnp.transpose(
            jnp.broadcast_to(delta, (rows, 128)), (1, 0))[0:1, :]
    stat[0, 0:heads, :] = lse_ref[...] * LOG2E

    d1 = go(doall.at[0], doall.at[1], down)
    s1 = go(stat.at[0], stat.at[1], down)
    d7 = go(doall.at[0], doall.at[7], up)
    s7 = go(stat.at[0], stat.at[7], up)

    def process(r, masked=False):
        def one(h, carry):
            keys = kall[h].reshape(4 * rows, width)
            values = vall[h].reshape(4 * rows, width)
            query = qall[r, h]
            grad = doall[r, h]
            total = stat[r, pl.ds(h, 1), :]
            delta = stat[r, pl.ds(heads + h, 1), :]
            raw = mm(keys, query, NT)
            shifted = raw * (factor * LOG2E) - total
            if masked:
                row = lax.broadcasted_iota(jnp.int32, shifted.shape, 0)
                col = lax.broadcasted_iota(jnp.int32, shifted.shape, 1)
                offs = []
                for j in range(4):
                    jx, jc = j // 2, j % 2
                    pj = (xb + jx) % 2 * 2 + (cb + jc) % 2
                    offs.append((pj - p - j) * rows)
                off = jnp.where(
                    row < 2 * rows,
                    jnp.where(row < rows, offs[0], offs[1]),
                    jnp.where(row < 3 * rows, offs[2], offs[3]))
                shifted = jnp.where(row + off <= col, shifted, -jnp.inf)
            prob = jnp.exp2(shifted)
            pgrad = mm(values, grad, NT)
            score = (prob * (pgrad - delta)).astype(BF)
            dvacc[h] += mm(prob.astype(BF), grad, NN)
            dkacc[h] += mm(score, query, NN)
            part = mm(score, keys, TN)
            if r == 0:
                dq0[h] = part
            else:
                dqb[r, h] = part.astype(BF)
            return carry

        lax.fori_loop(0, heads, one, 0)

    def guarded(r):
        @pl.when(z + r < Z)
        def _():
            process(r)

    process(0, masked=True)
    d1.wait_recv()
    d2 = go(doall.at[1], doall.at[2], down)
    s1.wait_recv()
    s2 = go(stat.at[1], stat.at[2], down)
    d7.wait_recv()
    d6 = go(doall.at[7], doall.at[6], up)
    s7.wait_recv()
    s6 = go(stat.at[7], stat.at[6], up)
    guarded(1)
    d2.wait_recv()
    d3 = go(doall.at[2], doall.at[3], down)
    s2.wait_recv()
    s3 = go(stat.at[2], stat.at[3], down)
    d6.wait_recv()
    d5 = go(doall.at[6], doall.at[5], up)
    s6.wait_recv()
    s5 = go(stat.at[6], stat.at[5], up)
    guarded(2)
    d3.wait_recv()
    d4a = go(doall.at[3, :, pl.ds(0, half)], doall.at[4, :, pl.ds(0, half)], down)
    s3.wait_recv()
    s4 = go(stat.at[3], stat.at[4], down)
    d5.wait_recv()
    d4b = go(doall.at[5, :, pl.ds(half, half)], doall.at[4, :, pl.ds(half, half)], up)
    s5.wait_recv()
    guarded(3)
    d4a.wait_recv()
    d4b.wait_recv()
    s4.wait_recv()
    guarded(4)

    def plus(a, b):
        return (a.astype(F32) + b.astype(F32)).astype(BF)

    lo, hi = pl.ds(0, half), pl.ds(half, half)
    r3 = go(dqb.at[4, :, lo], rbuf.at[3, :, lo], up)
    r5 = go(dqb.at[4, :, hi], rbuf.at[5, :, hi], down)
    guarded(5)
    r3.wait_recv()
    sbuf[3, :, :half] = plus(dqb[3, :, :half], rbuf[3, :, :half])
    sbuf[3, :, half:] = dqb[3, :, half:]
    r2 = go(sbuf.at[3], rbuf.at[2], up)
    r5.wait_recv()
    sbuf[5, :, half:] = plus(dqb[5, :, half:], rbuf[5, :, half:])
    sbuf[5, :, :half] = dqb[5, :, :half]
    r6 = go(sbuf.at[5], rbuf.at[6], down)
    guarded(6)
    r2.wait_recv()
    sbuf[2] = plus(dqb[2], rbuf[2])
    r1 = go(sbuf.at[2], rbuf.at[1], up)
    r6.wait_recv()
    sbuf[6] = plus(dqb[6], rbuf[6])
    r7 = go(sbuf.at[6], rbuf.at[7], down)
    guarded(7)

    for j, slot in ((0, 1), (1, 3)):
        at = pl.ds(slot * rows, rows)
        kv1s[j, 0] = dkacc[:, at, :].astype(BF)
        kv1s[j, 1] = dvacc[:, at, :].astype(BF)
    t1 = go(kv1s, kv1r, twin)
    r1.wait_recv()
    sbuf[1] = plus(dqb[1], rbuf[1])
    r0 = go(sbuf.at[1], rown.at[0], up)
    r7.wait_recv()
    sbuf[7] = plus(dqb[7], rbuf[7])
    r8 = go(sbuf.at[7], rown.at[1], down)
    t1.wait_recv()
    at = pl.ds(2 * rows, rows)
    kv2s[0] = (dkacc[:, at, :] + kv1r[1, 0].astype(F32)).astype(BF)
    kv2s[1] = (dvacc[:, at, :] + kv1r[1, 1].astype(F32)).astype(BF)
    t2 = go(kv2s, kv2r, side)
    at = pl.ds(0, rows)
    key_sum = dkacc[:, at, :] + kv1r[0, 0].astype(F32)
    value_sum = dvacc[:, at, :] + kv1r[0, 1].astype(F32)
    t2.wait_recv()
    dk_out[...] = ((key_sum + kv2r[0].astype(F32)) * factor).astype(BF)
    dv_out[...] = (value_sum + kv2r[1].astype(F32)).astype(BF)
    r0.wait_recv()
    r8.wait_recv()
    dq_out[...] = ((dq0[...] + rown[0].astype(F32) + rown[1].astype(F32)) * factor).astype(BF)

    for c in started:
        c.wait_send()


COPIES = 64


def body(queries, key_vectors, value_vectors, attn_output, output_grad, w_out, log_total):
    rows, heads, width = queries.shape
    major = lambda a: jnp.transpose(a, (1, 0, 2))
    block = jax.ShapeDtypeStruct((heads, rows, width), BF)
    vmem = pl.BlockSpec(memory_space=pltpu.VMEM)
    V = pltpu.VMEM
    blk = (heads, rows, width)
    outs = pl.pallas_call(
        kernel,
        out_shape=(block, block, block),
        in_specs=[vmem] * 6 + [pl.BlockSpec(memory_space=pl.ANY)],
        out_specs=(vmem, vmem, vmem),
        scratch_shapes=[
            V(w_out.shape, BF),
            V((2, Y) + output_grad.shape, BF),
            V((Z,) + blk, BF),
            V((heads, 4, rows, width), BF),
            V((heads, 4, rows, width), BF),
            V((Z,) + blk, BF),
            V((Z, 8, rows), F32),
            V((Z,) + blk, BF),
            V((Z,) + blk, BF),
            V((Z,) + blk, BF),
            V((2,) + blk, BF),
            V((heads, 4 * rows, width), F32),
            V((heads, 4 * rows, width), F32),
            V(blk, F32),
            V((2, 2) + blk, BF),
            V((2, 2) + blk, BF),
            V((2,) + blk, BF),
            V((2,) + blk, BF),
            pltpu.SemaphoreType.DMA,
            pltpu.SemaphoreType.DMA((COPIES,)),
            pltpu.SemaphoreType.DMA((COPIES,)),
        ],
        compiler_params=pltpu.CompilerParams(
            collective_id=0, has_side_effects=True, vmem_limit_bytes=60 * 1024 * 1024),
        name="attention_backward",
    )(
        major(queries), major(key_vectors), major(value_vectors), major(attn_output),
        output_grad, jnp.transpose(log_total, (1, 0)), w_out,
    )
    return tuple(major(a) for a in outs)


def solution(mesh):
    row = P("ctx", "head", None)
    return jax.shard_map(
        body, mesh=mesh,
        in_specs=(row, row, row, row, P("ctx", "head"), P("head", None), P("ctx", "head")),
        out_specs=(row, row, row), check_vma=False)
```

```python
import math

import jax
import jax.numpy as jnp
from jax import lax
from jax.experimental import pallas as pl
from jax.experimental.pallas import tpu as pltpu
from jax.sharding import PartitionSpec as P

MESH = pl.DeviceIdType.MESH
BF = jnp.bfloat16
F32 = jnp.float32
LOG2E = math.log2(math.e)
Z = 8
Y = 4
COPIES = 160

NT = (((1,), (1,)), ((), ()))
TN = (((0,), (0,)), ((), ()))
NN = (((1,), (0,)), ((), ()))


def mm(a, b, dims):
    return lax.dot_general(a, b, dims, preferred_element_type=F32)


def plus(a, b):
    return (a.astype(F32) + b.astype(F32)).astype(BF)


def kernel(
    q_ref, k_ref, v_ref, o_ref, g_ref, lse_ref, w_hbm,
    dq_out, dk_out, dv_out,
    w_vm, gall, qall, kall, vall, doall, stat, dqb, sbuf, rbuf, rown,
    dkacc, dvacc, dq0, kv1s, kv1r, kv2s, kv2r,
    w_sem, send_sem, recv_sem,
):
    heads, rows, width = q_ref.shape
    half = rows // 2
    factor = width ** -0.5
    ctx = lax.axis_index("ctx")
    hd = lax.axis_index("head")
    z = ctx // 4
    p = ctx % 4
    xb, cb = p // 2, p % 2
    xh, y = hd // Y, hd % Y

    def plane(to):
        return ((to + Z) % Z * 4 + p, hd)

    up, down = plane(z + 1), plane(z - 1)
    north = (ctx, xh * Y + (y + 1) % Y)
    south = (ctx, xh * Y + (y + Y - 1) % Y)
    across = (ctx, (1 - xh) * Y + y)
    side = (z * 4 + (1 - xb) * 2 + cb, hd)
    twin = (z * 4 + xb * 2 + 1 - cb, hd)
    peers = [plane(z + d) for d in (-3, -2, -1, 1, 2, 3)]
    peers += [north, south, across, side, twin]

    wcopy = pltpu.make_async_copy(w_hbm, w_vm, w_sem)
    wcopy.start()
    barrier = pltpu.get_barrier_semaphore()
    for peer in peers:
        pl.semaphore_signal(barrier, inc=1, device_id=peer, device_id_type=MESH)

    used = [0]
    channels = []

    def when(cond, act):
        if cond is None:
            act()
        else:
            pl.when(cond)(act)

    class Channel:
        def __init__(self, src, dst, to, send_if=None, recv_if=None, n=heads, shift=0, slots=None):
            self.src, self.dst, self.to, self.shift = src, dst, to, shift
            self.send_if, self.recv_if, self.n = send_if, recv_if, n
            self.base = used[0]
            used[0] += slots or n
            channels.append(self)

        def copy(self, i, shift):
            at = self.base + shift + i
            return pltpu.make_async_remote_copy(
                src_ref=self.src(i), dst_ref=self.dst(i),
                send_sem=send_sem.at[at], recv_sem=recv_sem.at[at],
                device_id=self.to, device_id_type=MESH)

        def start(self, i=0):
            when(self.send_if, lambda: self.copy(i, self.shift).start())

        def recv(self, i=0):
            when(self.recv_if, lambda: self.copy(i, 0).wait_recv())

        def recv_at(self, i, shift, cond):
            when(cond, lambda: self.copy(i, shift).wait_recv())

        def drain(self):
            def act():
                for i in range(self.n):
                    self.copy(i, self.shift).wait_send()
            when(self.send_if, act)

    def once(src, dst, to, **kw):
        return Channel(lambda i: src, lambda i: dst, to, n=1, **kw)

    def valid(r):
        return z + r <= Z - 1

    class Ring:
        def __init__(self, own, held, n):
            self.hops = {}
            for r in range(1, 5):
                src = own if r == 1 else (lambda i, r=r: held(r - 1, i))
                self.hops[r] = Channel(
                    src, lambda i, r=r: held(r, i), down, n=n,
                    send_if=(z >= 1) & (z - 1 + r <= Z - 1), recv_if=valid(r))
            self.wrap = Channel(
                own, lambda i: held(z, i), plane(0), n=n, send_if=z >= 5,
                shift=(z - 5) * n, slots=3 * n)
            self.seven = Channel(
                lambda i: held(7, i), lambda i: held(6, i), up, n=n,
                send_if=z == 0, recv_if=z == 1)
            self.six = Channel(
                lambda i: held(6, i), lambda i: held(5, i), up, n=n,
                send_if=z <= 1, recv_if=(z == 1) | (z == 2))
            self.n = n

        def begin(self):
            for i in range(self.n):
                self.hops[1].start(i)
                self.wrap.start(i)

        def recv(self, r, i):
            if r <= 4:
                self.hops[r].recv(i)
            else:
                self.wrap.recv_at(i, (r - 5) * self.n, z == 0)
                if r == 6:
                    self.seven.recv(i)
                if r == 5:
                    self.six.recv(i)

        def pass_on(self, r, i):
            if r < 4:
                self.hops[r + 1].start(i)
            if r == 7:
                self.seven.start(i)
            if r == 6:
                self.six.start(i)

    lo, hi = pl.ds(0, half), pl.ds(half, half)
    quarter = half // 2
    q_lo, q_mid = pl.ds(0, quarter), pl.ds(quarter, quarter)
    q_mid2, q_hi = pl.ds(half, quarter), pl.ds(half + quarter, quarter)

    g01 = [once(g_ref.at[s], gall.at[0, 1, s], south) for s in (lo, hi)]
    g03 = [once(g_ref.at[s], gall.at[0, 3, s], north) for s in (lo, hi)]
    g10 = [once(g_ref.at[s], gall.at[1, 0, s], across) for s in (lo, hi)]
    g02 = [once(gall.at[0, 1, lo], gall.at[0, 2, lo], south),
           once(gall.at[0, 3, hi], gall.at[0, 2, hi], north)]
    g11 = [once(gall.at[1, 0, s], gall.at[1, 1, s], south) for s in (lo, hi)]
    g13 = [once(gall.at[1, 0, s], gall.at[1, 3, s], north) for s in (lo, hi)]
    g12 = [once(gall.at[1, 1, q_lo], gall.at[1, 2, q_lo], south),
           once(gall.at[1, 3, q_hi], gall.at[1, 2, q_hi], north),
           once(gall.at[0, 2, q_mid], gall.at[1, 2, q_mid], across),
           once(gall.at[0, 2, q_mid2], gall.at[1, 2, q_mid2], across)]
    qring = Ring(lambda i: q_ref.at[i], lambda r, i: qall.at[r, i], heads)
    k2 = once(k_ref, kall.at[:, 2], side)
    v2 = once(v_ref, vall.at[:, 2], side)
    k1 = once(k_ref, kall.at[:, 1], twin)
    v1 = once(v_ref, vall.at[:, 1], twin)
    k3 = once(kall.at[:, 2], kall.at[:, 3], twin)
    v3 = once(vall.at[:, 2], vall.at[:, 3], twin)

    dkacc[...] = jnp.zeros_like(dkacc)
    dvacc[...] = jnp.zeros_like(dvacc)
    qall[0] = q_ref[...]
    kall[:, 0] = k_ref[...]
    vall[:, 0] = v_ref[...]
    pl.semaphore_wait(barrier, len(peers))

    g01[0].start()
    g03[1].start()
    g10[0].start()
    qring.begin()
    g01[1].start()
    g03[0].start()
    g10[1].start()
    k2.start()
    v2.start()
    k1.start()
    v1.start()
    wcopy.wait()

    def proj(a, b, block):
        at = ((xh + a) % 2 * Y + (y + b) % Y) * g_ref.shape[1]
        return mm(block, w_vm[:, pl.ds(pl.multiple_of(at, 128), g_ref.shape[1])], NT)

    acc = proj(0, 0, g_ref[...])
    for i in range(heads):
        qring.recv(1, i)
        qring.pass_on(1, i)
        if i == 1:
            g01[0].recv()
            g02[0].start()
            g03[1].recv()
            g02[1].start()
    g10[0].recv()
    g11[0].start()
    g13[0].start()
    for i in range(heads):
        qring.recv(2, i)
        qring.pass_on(2, i)
        qring.recv(7, i)
        qring.pass_on(7, i)
        if i == 1:
            g10[1].recv()
            g13[1].start()
            g11[1].start()
    g01[1].recv()
    g03[0].recv()
    acc += proj(0, 1, gall[0, 1])
    acc += proj(0, 3, gall[0, 3])
    acc += proj(1, 0, gall[1, 0])
    g02[0].recv()
    g12[2].start()
    g02[1].recv()
    g12[3].start()
    for i in range(heads):
        qring.recv(3, i)
        qring.pass_on(3, i)
        qring.recv(6, i)
        qring.pass_on(6, i)
    k2.recv()
    k3.start()
    v2.recv()
    v3.start()
    acc += proj(0, 2, gall[0, 2])
    g11[0].recv()
    g12[0].start()
    g13[1].recv()
    g12[1].start()
    g11[1].recv()
    g13[0].recv()
    acc += proj(1, 1, gall[1, 1])
    acc += proj(1, 3, gall[1, 3])
    for i in range(heads):
        qring.recv(4, i)
        qring.recv(5, i)
    k1.recv()
    v1.recv()
    k3.recv()
    v3.recv()
    for c in g12:
        c.recv()
    acc += proj(1, 2, gall[1, 2])

    grad = acc.astype(BF)
    stat[0] = jnp.zeros(stat.shape[1:], F32)
    for h in range(heads):
        grad_h = grad[:, h * width:(h + 1) * width]
        doall[0, h] = grad_h
        terms = grad_h.astype(F32) * o_ref[h].astype(F32)
        delta = jnp.sum(terms, axis=1, keepdims=True)
        stat[0, heads + h:heads + h + 1, :] = jnp.transpose(
            jnp.broadcast_to(delta, (rows, 128)), (1, 0))[0:1, :]
    stat[0, 0:heads, :] = lse_ref[...] * LOG2E

    sring = Ring(lambda i: stat.at[0], lambda r, i: stat.at[r], 1)
    dring = Ring(lambda i: doall.at[0, i], lambda r, i: doall.at[r, i], heads)
    sring.begin()
    dring.begin()

    def tile(r, h, masked=False):
        keys = kall[h].reshape(4 * rows, width)
        values = vall[h].reshape(4 * rows, width)
        query = qall[r, h]
        grad = doall[r, h]
        total = stat[r, pl.ds(h, 1), :]
        delta = stat[r, pl.ds(heads + h, 1), :]
        raw = mm(keys, query, NT)
        shifted = raw * (factor * LOG2E) - total
        if masked:
            row = lax.broadcasted_iota(jnp.int32, shifted.shape, 0)
            col = lax.broadcasted_iota(jnp.int32, shifted.shape, 1)
            offs = []
            for j in range(4):
                jx, jc = j // 2, j % 2
                pj = (xb + jx) % 2 * 2 + (cb + jc) % 2
                offs.append((pj - p - j) * rows)
            off = jnp.where(
                row < 2 * rows,
                jnp.where(row < rows, offs[0], offs[1]),
                jnp.where(row < 3 * rows, offs[2], offs[3]))
            shifted = jnp.where(row + off <= col, shifted, -jnp.inf)
        prob = jnp.exp2(shifted)
        pgrad = mm(values, grad, NT)
        score = (prob * (pgrad - delta)).astype(BF)
        dvacc[h] += mm(prob.astype(BF), grad, NN)
        dkacc[h] += mm(score, query, NN)
        part = mm(score, keys, TN)
        if r == 0:
            dq0[h] = part
        else:
            dqb[r, h] = part.astype(BF)

    def each(act):
        def one(h, carry):
            act(h)
            return carry
        lax.fori_loop(0, heads, one, 0)

    def take(r, h):
        if isinstance(h, int):
            first = h == 0
            if first:
                sring.recv(r, 0)
                sring.pass_on(r, 0)
        else:
            @pl.when(h == 0)
            def _():
                sring.recv(r, 0)
                sring.pass_on(r, 0)
        dring.recv(r, h)
        dring.pass_on(r, h)

    def guarded(r, h):
        pl.when(valid(r))(lambda: tile(r, h))

    part = lambda r: (lambda i: dqb.at[r, i])
    r2 = Channel(part(2), lambda i: rbuf.at[1, i], up, send_if=valid(2), recv_if=(z >= 1) & valid(1))
    r1 = Channel(lambda i: sbuf.at[1, i], lambda i: rown.at[1, i], up, send_if=valid(1), recv_if=z >= 1)
    r4 = Channel(part(4), lambda i: rbuf.at[3, i], up, send_if=valid(4), recv_if=(z >= 1) & valid(3))
    r3 = Channel(lambda i: sbuf.at[3, i], lambda i: rown.at[0, i], plane(z + 3), send_if=valid(3), recv_if=z >= 3)
    r5 = Channel(part(5), lambda i: rbuf.at[6, i], down, send_if=(z >= 1) & valid(5), recv_if=z <= 1)
    r6 = Channel(lambda i: sbuf.at[6, i], lambda i: rbuf.at[7, i], down, send_if=z == 1, recv_if=z == 0)
    last = {
        r: Channel(src, lambda i: rown.at[2, i], plane(r), send_if=z == 0, recv_if=z == r)
        for r, src in ((5, part(5)), (6, lambda i: sbuf.at[6, i]), (7, lambda i: sbuf.at[7, i]))
    }
    t1 = Channel(lambda i: kv1s.at[i], lambda i: kv1r.at[i], twin)
    t2 = Channel(lambda i: kv2s.at[i], lambda i: kv2r.at[i], side)

    each(lambda h: tile(0, h, masked=True))

    def stage1(h):
        take(1, h)
        guarded(1, h)

    each(stage1)

    def stage7(h):
        take(7, h)
        guarded(7, h)

    each(stage7)

    def stage2(h):
        take(2, h)
        take(6, h)
        guarded(2, h)
        r2.start(h)

    each(stage2)

    def stage5(h):
        take(3, h)
        take(5, h)
        guarded(5, h)
        r5.start(h)
        last[5].start(h)

    each(stage5)

    def stage3(h):
        guarded(3, h)
        r2.recv(h)

        @pl.when(z >= 1)
        def _():
            sbuf[1, h] = plus(dqb[1, h], rbuf[1, h])

        @pl.when(z == 0)
        def _():
            sbuf[1, h] = dqb[1, h]

        r1.start(h)

    each(stage3)

    def stage4(h):
        take(4, h)
        guarded(4, h)
        r4.start(h)

    each(stage4)

    def stage6(h):
        guarded(6, h)
        for j, slot in ((0, 1), (1, 3)):
            at = pl.ds(slot * rows, rows)
            kv1s[h, j, 0] = dkacc[h, at, :].astype(BF)
            kv1s[h, j, 1] = dvacc[h, at, :].astype(BF)
        t1.start(h)
        r4.recv(h)

        @pl.when(z >= 1)
        def _():
            sbuf[3, h] = plus(dqb[3, h], rbuf[3, h])

        @pl.when(z == 0)
        def _():
            sbuf[3, h] = dqb[3, h]

        r3.start(h)
        r5.recv(h)

        @pl.when(z <= 1)
        def _():
            sbuf[6, h] = plus(dqb[6, h], rbuf[6, h])

        r6.start(h)
        last[6].start(h)

    each(stage6)

    def fold(h):
        t1.recv(h)
        at = pl.ds(2 * rows, rows)
        kv2s[h, 0] = plus(dkacc[h, at, :], kv1r[h, 1, 0])
        kv2s[h, 1] = plus(dvacc[h, at, :], kv1r[h, 1, 1])
        t2.start(h)
        r6.recv(h)

        @pl.when(z == 0)
        def _():
            sbuf[7, h] = plus(dqb[7, h], rbuf[7, h])

        last[7].start(h)

    each(fold)

    def finish(h):
        t2.recv(h)
        at = pl.ds(0, rows)
        key_sum = dkacc[h, at, :] + kv1r[h, 0, 0].astype(F32) + kv2r[h, 0].astype(F32)
        value_sum = dvacc[h, at, :] + kv1r[h, 0, 1].astype(F32) + kv2r[h, 1].astype(F32)
        dk_out[h] = (key_sum * factor).astype(BF)
        dv_out[h] = value_sum.astype(BF)
        r1.recv(h)
        r3.recv(h)
        for r in (5, 6, 7):
            last[r].recv(h)
        for slot, cond in ((1, z >= 1), (0, z >= 3), (2, z >= 5)):
            @pl.when(cond)
            def _(slot=slot):
                dq0[h] += rown[slot, h].astype(F32)
        dq_out[h] = (dq0[h] * factor).astype(BF)

    each(finish)

    for c in channels:
        c.drain()


def body(queries, key_vectors, value_vectors, attn_output, output_grad, w_out, log_total):
    rows, heads, width = queries.shape
    major = lambda a: jnp.transpose(a, (1, 0, 2))
    block = jax.ShapeDtypeStruct((heads, rows, width), BF)
    vmem = pl.BlockSpec(memory_space=pltpu.VMEM)
    V = pltpu.VMEM
    blk = (heads, rows, width)
    outs = pl.pallas_call(
        kernel,
        out_shape=(block, block, block),
        in_specs=[vmem] * 6 + [pl.BlockSpec(memory_space=pl.ANY)],
        out_specs=(vmem, vmem, vmem),
        scratch_shapes=[
            V(w_out.shape, BF),
            V((2, Y) + output_grad.shape, BF),
            V((Z,) + blk, BF),
            V((heads, 4, rows, width), BF),
            V((heads, 4, rows, width), BF),
            V((Z,) + blk, BF),
            V((Z, 8, rows), F32),
            V((Z,) + blk, BF),
            V((Z,) + blk, BF),
            V((Z,) + blk, BF),
            V((3,) + blk, BF),
            V((heads, 4 * rows, width), F32),
            V((heads, 4 * rows, width), F32),
            V(blk, F32),
            V((heads, 2, 2, rows, width), BF),
            V((heads, 2, 2, rows, width), BF),
            V((heads, 2, rows, width), BF),
            V((heads, 2, rows, width), BF),
            pltpu.SemaphoreType.DMA,
            pltpu.SemaphoreType.DMA((COPIES,)),
            pltpu.SemaphoreType.DMA((COPIES,)),
        ],
        compiler_params=pltpu.CompilerParams(
            collective_id=0, has_side_effects=True, vmem_limit_bytes=60 * 1024 * 1024),
        name="attention_backward",
    )(
        major(queries), major(key_vectors), major(value_vectors), major(attn_output),
        output_grad, jnp.transpose(log_total, (1, 0)), w_out,
    )
    return tuple(major(a) for a in outs)


def solution(mesh):
    row = P("ctx", "head", None)
    return jax.shard_map(
        body, mesh=mesh,
        in_specs=(row, row, row, row, P("ctx", "head"), P("head", None), P("ctx", "head")),
        out_specs=(row, row, row), check_vma=False)
```

```python
import math

import jax
import jax.numpy as jnp
from jax import lax
from jax.experimental import pallas as pl
from jax.experimental.pallas import tpu as pltpu
from jax.sharding import PartitionSpec as P

MESH = pl.DeviceIdType.MESH
BF = jnp.bfloat16
F32 = jnp.float32
LOG2E = math.log2(math.e)
Z = 8
Y = 4
COPIES = 320

NT = (((1,), (1,)), ((), ()))
TN = (((0,), (0,)), ((), ()))
NN = (((1,), (0,)), ((), ()))


def mm(a, b, dims):
    return lax.dot_general(a, b, dims, preferred_element_type=F32)


def plus(a, b):
    return (a.astype(F32) + b.astype(F32)).astype(BF)


def kernel(
    q_ref, k_ref, v_ref, o_ref, g_ref, lse_ref, w_hbm,
    out,
    w_vm, gall, qall, kall, vall, doall, tots, dels, probs, dqb, sbuf, rbuf, rown,
    dkacc, dvacc, dq0, kv1s, kv1r, kv2s, kv2r,
    w_sem, send_sem, recv_sem,
):
    heads, rows, width = q_ref.shape
    half = rows // 2
    factor = width ** -0.5
    ctx = lax.axis_index("ctx")
    hd = lax.axis_index("head")
    z = ctx // 4
    p = ctx % 4
    xb, cb = p // 2, p % 2
    xh, y = hd // Y, hd % Y

    def plane(to):
        return ((to + Z) % Z * 4 + p, hd)

    up, down = plane(z + 1), plane(z - 1)
    north = (ctx, xh * Y + (y + 1) % Y)
    south = (ctx, xh * Y + (y + Y - 1) % Y)
    across = (ctx, (1 - xh) * Y + y)
    side = (z * 4 + (1 - xb) * 2 + cb, hd)
    twin = (z * 4 + xb * 2 + 1 - cb, hd)
    peers = [plane(z + d) for d in (-3, -2, -1, 1, 2, 3)]
    peers += [north, south, across, side, twin]

    wcopy = pltpu.make_async_copy(w_hbm, w_vm, w_sem)
    wcopy.start()
    barrier = pltpu.get_barrier_semaphore()
    for peer in peers:
        pl.semaphore_signal(barrier, inc=1, device_id=peer, device_id_type=MESH)

    used = [0]
    channels = []

    def when(cond, act):
        if cond is None:
            act()
        else:
            pl.when(cond)(act)

    class Channel:
        def __init__(self, src, dst, to, send_if=None, recv_if=None, waves=2, m=heads, shift=0, slots=1):
            self.src, self.dst, self.to, self.shift = src, dst, to, shift
            self.send_if, self.recv_if, self.waves, self.m = send_if, recv_if, waves, m
            self.base = used[0]
            used[0] += waves * m * slots
            channels.append(self)

        def copy(self, w, h, shift):
            at = self.base + shift + w * self.m + h
            return pltpu.make_async_remote_copy(
                src_ref=self.src(w, h), dst_ref=self.dst(w, h),
                send_sem=send_sem.at[at], recv_sem=recv_sem.at[at],
                device_id=self.to, device_id_type=MESH)

        def start(self, w=0, h=0):
            when(self.send_if, lambda: self.copy(w, h, self.shift).start())

        def recv(self, w=0, h=0):
            when(self.recv_if, lambda: self.copy(w, h, 0).wait_recv())

        def recv_at(self, w, h, shift, cond):
            when(cond, lambda: self.copy(w, h, shift).wait_recv())

        def drain(self):
            def act():
                for w in range(self.waves):
                    for h in range(self.m):
                        self.copy(w, h, self.shift).wait_send()
            when(self.send_if, act)

    def once(src, dst, to, **kw):
        return Channel(lambda w, h: src, lambda w, h: dst, to, waves=1, m=1, **kw)

    def valid(r):
        return z + r <= Z - 1

    class Ring:
        def __init__(self, own, held, m):
            self.hops = {}
            self.m = m
            for r in range(1, 5):
                src = own if r == 1 else (lambda w, h, r=r: held(r - 1, w, h))
                self.hops[r] = Channel(
                    src, lambda w, h, r=r: held(r, w, h), down, m=m,
                    send_if=(z >= 1) & (z - 1 + r <= Z - 1), recv_if=valid(r))
            self.wrap = Channel(
                own, lambda w, h: held(z, w, h), plane(0), m=m, send_if=z >= 5,
                shift=(z - 5) * 2 * m, slots=3)
            self.seven = Channel(
                lambda w, h: held(7, w, h), lambda w, h: held(6, w, h), up, m=m,
                send_if=z == 0, recv_if=z == 1)
            self.six = Channel(
                lambda w, h: held(6, w, h), lambda w, h: held(5, w, h), up, m=m,
                send_if=z <= 1, recv_if=(z == 1) | (z == 2))

        def begin(self, w):
            for h in range(self.m):
                self.hops[1].start(w, h)
                self.wrap.start(w, h)

        def step(self, r, w, h):
            if r <= 4:
                self.hops[r].recv(w, h)
                if r < 4:
                    self.hops[r + 1].start(w, h)
            else:
                self.wrap.recv_at(w, h, (r - 5) * 2 * self.m, z == 0)
                if r == 7:
                    self.seven.start(w, h)
                if r == 6:
                    self.seven.recv(w, h)
                    self.six.start(w, h)
                if r == 5:
                    self.six.recv(w, h)

        def hop(self, r, w):
            for h in range(self.m):
                self.step(r, w, h)

    def cut(w, first, size):
        return pl.ds(w * half + first * half // 4, size * half // 4)

    g01 = [once(g_ref.at[cut(w, 0, 4)], gall.at[0, 1, cut(w, 0, 4)], south) for w in (0, 1)]
    g03 = [once(g_ref.at[cut(w, 0, 4)], gall.at[0, 3, cut(w, 0, 4)], north) for w in (0, 1)]
    g10 = [once(g_ref.at[cut(w, 0, 4)], gall.at[1, 0, cut(w, 0, 4)], across) for w in (0, 1)]
    g02s = [once(gall.at[0, 1, cut(w, 0, 2)], gall.at[0, 2, cut(w, 0, 2)], south) for w in (0, 1)]
    g02n = [once(gall.at[0, 3, cut(w, 2, 2)], gall.at[0, 2, cut(w, 2, 2)], north) for w in (0, 1)]
    g11 = [once(gall.at[1, 0, cut(w, 0, 4)], gall.at[1, 1, cut(w, 0, 4)], south) for w in (0, 1)]
    g13 = [once(gall.at[1, 0, cut(w, 0, 4)], gall.at[1, 3, cut(w, 0, 4)], north) for w in (0, 1)]
    g12s = [once(gall.at[1, 1, cut(w, 0, 1)], gall.at[1, 2, cut(w, 0, 1)], south) for w in (0, 1)]
    g12x = [once(gall.at[0, 2, cut(w, 1, 2)], gall.at[1, 2, cut(w, 1, 2)], across) for w in (0, 1)]
    g12n = [once(gall.at[1, 3, cut(w, 3, 1)], gall.at[1, 2, cut(w, 3, 1)], north) for w in (0, 1)]
    at_rows = lambda w: pl.ds(w * half, half)
    qring = Ring(lambda w, h: q_ref.at[h, at_rows(w)], lambda r, w, h: qall.at[r, w * heads + h], heads)
    lring = Ring(lambda w, h: tots.at[0, w], lambda r, w, h: tots.at[r, w], 1)
    k2 = once(k_ref, kall.at[:, 2], side)
    v2 = once(v_ref, vall.at[:, 2], side)
    k1 = once(k_ref, kall.at[:, 1], twin)
    v1 = once(v_ref, vall.at[:, 1], twin)
    k3 = once(kall.at[:, 2], kall.at[:, 3], twin)
    v3 = once(vall.at[:, 2], vall.at[:, 3], twin)

    dkacc[...] = jnp.zeros_like(dkacc)
    dvacc[...] = jnp.zeros_like(dvacc)
    for w in (0, 1):
        for h in range(heads):
            qall[0, w * heads + h] = q_ref[h, w * half:(w + 1) * half]
    kall[:, 0] = k_ref[...]
    vall[:, 0] = v_ref[...]
    for r in (1, 3, 5, 7):
        @pl.when(z + r >= Z)
        def _(r=r):
            qall[r] = jnp.zeros(qall.shape[1:], BF)
            doall[r] = jnp.zeros(doall.shape[1:], BF)
            tots[r] = jnp.zeros(tots.shape[1:], F32)
            dels[r] = jnp.zeros(dels.shape[1:], F32)
    for w in (0, 1):
        tots[0, w] = jnp.zeros(tots.shape[2:], F32)
        tots[0, w, 0:heads, :] = lse_ref[:, w * half:(w + 1) * half] * LOG2E
    pl.semaphore_wait(barrier, len(peers))

    sring = Ring(lambda w, h: dels.at[0, w], lambda r, w, h: dels.at[r, w], 1)
    dring = Ring(lambda w, h: doall.at[0, w * heads + h], lambda r, w, h: doall.at[r, w * heads + h], heads)

    def hop(r, w):
        sring.hop(r, w)
        dring.hop(r, w)

    def qhop(r, w):
        lring.hop(r, w)
        qring.hop(r, w)

    def proj(a, b, w):
        at = ((xh + a) % 2 * Y + (y + b) % Y) * g_ref.shape[1]
        block = g_ref[w * half:(w + 1) * half] if a == b == 0 else gall[a, b, w * half:(w + 1) * half]
        return mm(block, w_vm[:, pl.ds(pl.multiple_of(at, 128), g_ref.shape[1])], NT)

    def project(w):
        grad = acc[w].astype(BF)
        dels[0, w] = jnp.zeros(dels.shape[2:], F32)
        for h in range(heads):
            grad_h = grad[:, h * width:(h + 1) * width]
            doall[0, w * heads + h] = grad_h
            terms = grad_h.astype(F32) * o_ref[h, w * half:(w + 1) * half].astype(F32)
            delta = jnp.sum(terms, axis=1, keepdims=True)
            dels[0, w, h:h + 1, :] = jnp.transpose(
                jnp.broadcast_to(delta, (half, 128)), (1, 0))[0:1, :]
        sring.begin(w)
        dring.begin(w)

    def line(ref, a, w, h):
        return jnp.concatenate([ref[a, w, pl.ds(h, 1), :], ref[a + 1, w, pl.ds(h, 1), :]], axis=1)

    def both(ref, a, w, h):
        i = w * heads + h
        return jnp.concatenate([ref[a, i], ref[a + 1, i]], axis=0)

    def prob_of(a, w, h):
        keys = kall[h].reshape(4 * rows, width)
        raw = mm(keys, both(qall, a, w, h), NT)
        shifted = raw * (factor * LOG2E) - line(tots, a, w, h)
        if a == 0:
            row = lax.broadcasted_iota(jnp.int32, shifted.shape, 0)
            col = lax.broadcasted_iota(jnp.int32, shifted.shape, 1)
            offs = []
            for j in range(4):
                jx, jc = j // 2, j % 2
                pj = (xb + jx) % 2 * 2 + (cb + jc) % 2
                offs.append((pj - p - j) * rows)
            off = jnp.where(
                row < 2 * rows,
                jnp.where(row < rows, offs[0], offs[1]),
                jnp.where(row < 3 * rows, offs[2], offs[3]))
            shown = (row + off <= col + w * half) | (col >= half)
            shifted = jnp.where(shown, shifted, -jnp.inf)
        return jnp.exp2(shifted)

    def front(a, w, h):
        probs[a + w, h] = prob_of(a, w, h)

    def tile(a, w, h):
        i = w * heads + h
        keys = kall[h].reshape(4 * rows, width)
        values = vall[h].reshape(4 * rows, width)
        query = both(qall, a, w, h)
        grad = both(doall, a, w, h)
        prob = probs[a + w, h] if a <= 2 else prob_of(a, w, h)
        pgrad = mm(values, grad, NT)
        score = (prob * (pgrad - line(dels, a, w, h))).astype(BF)
        dvacc[h] += mm(prob.astype(BF), grad, NN)
        dkacc[h] += mm(score, query, NN)
        part = mm(score, keys, TN)
        if a == 0:
            dq0[i] = part[:half]
        else:
            dqb[a, i] = part[:half].astype(BF)
        dqb[a + 1, i] = part[half:].astype(BF)

    def each(act):
        def one(h, carry):
            act(h)
            return carry
        lax.fori_loop(0, heads, one, 0)

    def serve(hops, h):
        if hops:
            @pl.when(h == 0)
            def _():
                for r, w in hops:
                    sring.hop(r, w)
            for r, w in hops:
                dring.step(r, w, h)

    def fronts(a, w, hops=()):
        def act(h):
            serve(hops, h)
            if a == 0:
                front(a, w, h)
            else:
                pl.when(valid(a))(lambda: front(a, w, h))
        each(act)

    def tiles(a, w, hops=(), then=None):
        def act(h):
            serve(hops, h)
            if a == 0:
                tile(a, w, h)
            else:
                pl.when(valid(a))(lambda: tile(a, w, h))
            if then is not None:
                then(h)
        each(act)

    def of(ref, r):
        return lambda w, h: ref.at[r, w * heads + h]

    r2 = Channel(of(dqb, 2), of(rbuf, 1), up, send_if=valid(2), recv_if=(z >= 1) & valid(1))
    r1 = Channel(of(sbuf, 1), of(rown, 1), up, send_if=valid(1), recv_if=z >= 1)
    r4 = Channel(of(dqb, 4), of(rbuf, 3), up, send_if=valid(4), recv_if=(z >= 1) & valid(3))
    r3 = Channel(of(sbuf, 3), of(rown, 0), plane(z + 3), send_if=valid(3), recv_if=z >= 3)
    wrapped = {
        r: Channel(
            of(dqb, r), lambda w, h: rown.at[2 + z % 5, w * heads + h], plane(z + r),
            send_if=valid(r), recv_if=z >= r)
        for r in (5, 6, 7)
    }
    t1 = Channel(lambda w, h: kv1s.at[h], lambda w, h: kv1r.at[h], twin, waves=1)
    t2 = Channel(lambda w, h: kv2s.at[h], lambda w, h: kv2r.at[h], side, waves=1)

    def merge(r, w, h, got, alone):
        i = w * heads + h

        @pl.when(got)
        def _():
            sbuf[r, i] = plus(dqb[r, i], rbuf[r, i])

        if alone is not None:
            @pl.when(alone)
            def _():
                sbuf[r, i] = dqb[r, i]

    def near(w):
        def act(h):
            r2.recv(w, h)
            merge(1, w, h, z >= 1, z == 0)
            r1.start(w, h)
        each(act)

    def far(w):
        def act(h):
            r4.recv(w, h)
            merge(3, w, h, z >= 1, z == 0)
            r3.start(w, h)
        each(act)

    def send2(w):
        return lambda h: r2.start(w, h)

    def send45(w):
        def then(h):
            r4.start(w, h)
            wrapped[5].start(w, h)
        return then

    def send67(w):
        def then(h):
            wrapped[6].start(w, h)
            wrapped[7].start(w, h)
        return then

    def hand_over(h):
        send67(1)(h)
        for j, slot in ((0, 1), (1, 3)):
            at = pl.ds(slot * rows, rows)
            kv1s[h, j, 0] = dkacc[h, at, :].astype(BF)
            kv1s[h, j, 1] = dvacc[h, at, :].astype(BF)
        t1.start(0, h)

    def fold(h):
        t1.recv(0, h)
        at = pl.ds(2 * rows, rows)
        kv2s[h, 0] = plus(dkacc[h, at, :], kv1r[h, 1, 0])
        kv2s[h, 1] = plus(dvacc[h, at, :], kv1r[h, 1, 1])
        t2.start(0, h)

    g01[0].start()
    g03[0].start()
    g10[0].start()
    lring.begin(0)
    qring.begin(0)
    g01[1].start()
    g03[1].start()
    g10[1].start()
    lring.begin(1)
    qring.begin(1)
    k2.start()
    k1.start()
    v2.start()
    v1.start()
    wcopy.wait()

    acc = [proj(0, 0, 0), proj(0, 0, 1)]
    qhop(1, 0)
    g01[0].recv()
    g02s[0].start()
    g03[0].recv()
    g02n[0].start()
    g10[0].recv()
    g11[0].start()
    g13[0].start()
    qhop(1, 1)
    acc[0] += proj(0, 1, 0)
    acc[0] += proj(0, 3, 0)
    acc[0] += proj(1, 0, 0)
    g01[1].recv()
    g02s[1].start()
    g03[1].recv()
    g02n[1].start()
    qhop(2, 0)
    g02s[0].recv()
    g02n[0].recv()
    g12x[0].start()
    qhop(2, 1)
    k1.recv()
    k2.recv()
    k3.start()
    acc[0] += proj(0, 2, 0)
    acc[1] += proj(0, 1, 1)
    acc[1] += proj(0, 3, 1)
    qhop(3, 0)
    g11[0].recv()
    g12s[0].start()
    g13[0].recv()
    g12n[0].start()
    g10[1].recv()
    g11[1].start()
    g13[1].start()
    acc[0] += proj(1, 1, 0)
    acc[0] += proj(1, 3, 0)
    acc[1] += proj(1, 0, 1)
    k3.recv()
    fronts(0, 0)
    qhop(3, 1)
    g02s[1].recv()
    g02n[1].recv()
    g12x[1].start()
    for c in (g12s[0], g12n[0], g12x[0]):
        c.recv()
    acc[0] += proj(1, 2, 0)
    project(0)
    v2.recv()
    v3.start()
    g11[1].recv()
    g12s[1].start()
    g13[1].recv()
    g12n[1].start()
    qhop(7, 0)
    qhop(7, 1)
    fronts(0, 1)
    acc[1] += proj(0, 2, 1)
    acc[1] += proj(1, 1, 1)
    acc[1] += proj(1, 3, 1)
    hop(1, 0)
    for c in (g12s[1], g12n[1], g12x[1]):
        c.recv()
    acc[1] += proj(1, 2, 1)
    project(1)
    v1.recv()
    v3.recv()
    fronts(2, 0, [(2, 0)])
    qhop(6, 0)
    qhop(6, 1)
    qhop(4, 0)
    tiles(0, 0, [(1, 1)])
    fronts(2, 1, [(3, 0)])
    tiles(2, 0, [(7, 0), (2, 1)], send2(0))
    qhop(5, 0)
    qhop(4, 1)
    tiles(0, 1, [(4, 0), (6, 0)])
    qhop(5, 1)
    tiles(4, 0, [(3, 1), (5, 0)], send45(0))
    tiles(2, 1, [(7, 1)], send2(1))
    near(0)
    tiles(6, 0, [(4, 1), (6, 1)], send67(0))
    far(0)

    def final(h):
        serve([(5, 1)], h)
        pl.when(valid(4))(lambda: tile(4, 1, h))
        send45(1)(h)
        pl.when(valid(6))(lambda: tile(6, 1, h))
        hand_over(h)

        @pl.when(h > 0)
        def _():
            fold(h - 1)

    each(final)
    fold(heads - 1)
    near(1)
    far(1)

    def finish(h):
        for w in (0, 1):
            i = w * heads + h
            r1.recv(w, h)
            r3.recv(w, h)
            for r in (5, 6, 7):
                wrapped[r].recv(w, h)
            for slot, cond in ((1, z >= 1), (0, z >= 3)) + tuple((2 + z - r, z >= r) for r in (5, 6, 7)):
                @pl.when(cond)
                def _(slot=slot, i=i):
                    dq0[i] += rown[slot, i].astype(F32)
            out[0, h, at_rows(w)] = (dq0[i] * factor).astype(BF)
        t2.recv(0, h)
        at = pl.ds(0, rows)
        key_sum = dkacc[h, at, :] + kv1r[h, 0, 0].astype(F32) + kv2r[h, 0].astype(F32)
        value_sum = dvacc[h, at, :] + kv1r[h, 0, 1].astype(F32) + kv2r[h, 1].astype(F32)
        out[1, h] = (key_sum * factor).astype(BF)
        out[2, h] = value_sum.astype(BF)

    each(finish)

    for c in channels:
        c.drain()


def body(queries, key_vectors, value_vectors, attn_output, output_grad, w_out, log_total):
    rows, heads, width = queries.shape
    major = lambda a: jnp.transpose(a, (1, 0, 2))
    vmem = pl.BlockSpec(memory_space=pltpu.VMEM)
    V = pltpu.VMEM
    blk = (heads, rows, width)
    chunks = (2 * heads, rows // 2, width)
    outs = pl.pallas_call(
        kernel,
        out_shape=jax.ShapeDtypeStruct((3,) + blk, BF),
        in_specs=[vmem] * 6 + [pl.BlockSpec(memory_space=pl.ANY)],
        out_specs=vmem,
        scratch_shapes=[
            V(w_out.shape, BF),
            V((2, Y) + output_grad.shape, BF),
            V((Z,) + chunks, BF),
            V((heads, 4, rows, width), BF),
            V((heads, 4, rows, width), BF),
            V((Z,) + chunks, BF),
            V((Z, 2, 8, rows // 2), F32),
            V((Z, 2, 8, rows // 2), F32),
            V((4, heads, 4 * rows, rows), F32),
            V((Z,) + chunks, BF),
            V((Z,) + chunks, BF),
            V((Z,) + chunks, BF),
            V((5,) + chunks, BF),
            V((heads, 4 * rows, width), F32),
            V((heads, 4 * rows, width), F32),
            V(chunks, F32),
            V((heads, 2, 2, rows, width), BF),
            V((heads, 2, 2, rows, width), BF),
            V((heads, 2, rows, width), BF),
            V((heads, 2, rows, width), BF),
            pltpu.SemaphoreType.DMA,
            pltpu.SemaphoreType.DMA((COPIES,)),
            pltpu.SemaphoreType.DMA((COPIES,)),
        ],
        compiler_params=pltpu.CompilerParams(
            collective_id=0, has_side_effects=True, vmem_limit_bytes=60 * 1024 * 1024),
        name="attention_backward",
    )(
        major(queries), major(key_vectors), major(value_vectors), major(attn_output),
        output_grad, jnp.transpose(log_total, (1, 0)), w_out,
    )
    return tuple(major(outs[i]) for i in range(3))


def solution(mesh):
    row = P("ctx", "head", None)
    return jax.shard_map(
        body, mesh=mesh,
        in_specs=(row, row, row, row, P("ctx", "head"), P("head", None), P("ctx", "head")),
        out_specs=(row, row, row), check_vma=False)
```

```python
import math

import jax
import jax.numpy as jnp
from jax import lax
from jax.experimental import pallas as pl
from jax.experimental.pallas import tpu as pltpu
from jax.sharding import PartitionSpec as P

MESH = pl.DeviceIdType.MESH
BF = jnp.bfloat16
F32 = jnp.float32
LOG2E = math.log2(math.e)
Z = 8
Y = 4
COPIES = 320

NT = (((1,), (1,)), ((), ()))
TN = (((0,), (0,)), ((), ()))
NN = (((1,), (0,)), ((), ()))


def mm(a, b, dims):
    return lax.dot_general(a, b, dims, preferred_element_type=F32)


def plus(a, b):
    return (a.astype(F32) + b.astype(F32)).astype(BF)


def kernel(
    q_ref, k_ref, v_ref, o_ref, g_ref, lse_ref, w_hbm,
    out,
    w_vm, gall, qall, kall, vall, doall, tots, dels, probs, dqb, sbuf, rbuf, rown,
    dkacc, dvacc, dq0, kv1s, kv1r, kv2s, kv2r,
    w_sem, send_sem, recv_sem,
):
    heads, rows, width = q_ref.shape
    half = rows // 2
    factor = width ** -0.5
    ctx = lax.axis_index("ctx")
    hd = lax.axis_index("head")
    z = ctx // 4
    p = ctx % 4
    xb, cb = p // 2, p % 2
    xh, y = hd // Y, hd % Y

    def plane(to):
        return ((to + Z) % Z * 4 + p, hd)

    up, down = plane(z + 1), plane(z - 1)
    north = (ctx, xh * Y + (y + 1) % Y)
    south = (ctx, xh * Y + (y + Y - 1) % Y)
    across = (ctx, (1 - xh) * Y + y)
    side = (z * 4 + (1 - xb) * 2 + cb, hd)
    twin = (z * 4 + xb * 2 + 1 - cb, hd)
    peers = [plane(z + d) for d in (-3, -2, -1, 1, 2, 3)]
    peers += [north, south, across, side, twin]

    wcopy = pltpu.make_async_copy(w_hbm, w_vm, w_sem)
    wcopy.start()
    barrier = pltpu.get_barrier_semaphore()
    for peer in peers:
        pl.semaphore_signal(barrier, inc=1, device_id=peer, device_id_type=MESH)

    used = [0]
    channels = []

    def when(cond, act):
        if cond is None:
            act()
        else:
            pl.when(cond)(act)

    class Channel:
        def __init__(self, src, dst, to, send_if=None, recv_if=None, waves=2, m=heads, shift=0, slots=1):
            self.src, self.dst, self.to, self.shift = src, dst, to, shift
            self.send_if, self.recv_if, self.waves, self.m = send_if, recv_if, waves, m
            self.base = used[0]
            used[0] += waves * m * slots
            channels.append(self)

        def copy(self, w, h, shift):
            at = self.base + shift + w * self.m + h
            return pltpu.make_async_remote_copy(
                src_ref=self.src(w, h), dst_ref=self.dst(w, h),
                send_sem=send_sem.at[at], recv_sem=recv_sem.at[at],
                device_id=self.to, device_id_type=MESH)

        def start(self, w=0, h=0):
            when(self.send_if, lambda: self.copy(w, h, self.shift).start())

        def recv(self, w=0, h=0):
            when(self.recv_if, lambda: self.copy(w, h, 0).wait_recv())

        def recv_at(self, w, h, shift, cond):
            when(cond, lambda: self.copy(w, h, shift).wait_recv())

        def drain(self):
            def act():
                for w in range(self.waves):
                    for h in range(self.m):
                        self.copy(w, h, self.shift).wait_send()
            when(self.send_if, act)

    def once(src, dst, to, **kw):
        return Channel(lambda w, h: src, lambda w, h: dst, to, waves=1, m=1, **kw)

    def valid(r):
        return z + r <= Z - 1

    class Ring:
        def __init__(self, own, held, m):
            self.hops = {}
            self.m = m
            for r in range(1, 5):
                src = own if r == 1 else (lambda w, h, r=r: held(r - 1, w, h))
                self.hops[r] = Channel(
                    src, lambda w, h, r=r: held(r, w, h), down, m=m,
                    send_if=(z >= 1) & (z - 1 + r <= Z - 1), recv_if=valid(r))
            self.wrap = Channel(
                own, lambda w, h: held(z, w, h), plane(0), m=m, send_if=z >= 5,
                shift=(z - 5) * 2 * m, slots=3)
            self.seven = Channel(
                lambda w, h: held(7, w, h), lambda w, h: held(6, w, h), up, m=m,
                send_if=z == 0, recv_if=z == 1)
            self.six = Channel(
                lambda w, h: held(6, w, h), lambda w, h: held(5, w, h), up, m=m,
                send_if=z <= 1, recv_if=(z == 1) | (z == 2))

        def begin(self, w):
            for h in range(self.m):
                self.hops[1].start(w, h)
                self.wrap.start(w, h)

        def step(self, r, w, h):
            if r <= 4:
                self.hops[r].recv(w, h)
                if r < 4:
                    self.hops[r + 1].start(w, h)
            else:
                self.wrap.recv_at(w, h, (r - 5) * 2 * self.m, z == 0)
                if r == 7:
                    self.seven.start(w, h)
                if r == 6:
                    self.seven.recv(w, h)
                    self.six.start(w, h)
                if r == 5:
                    self.six.recv(w, h)

        def hop(self, r, w):
            for h in range(self.m):
                self.step(r, w, h)

    def cut(w, first, size):
        return pl.ds(w * half + first * half // 4, size * half // 4)

    g01 = [once(g_ref.at[cut(w, 0, 4)], gall.at[0, 1, cut(w, 0, 4)], south) for w in (0, 1)]
    g03 = [once(g_ref.at[cut(w, 0, 4)], gall.at[0, 3, cut(w, 0, 4)], north) for w in (0, 1)]
    g10 = [once(g_ref.at[cut(w, 0, 4)], gall.at[1, 0, cut(w, 0, 4)], across) for w in (0, 1)]
    g02s = [once(gall.at[0, 1, cut(w, 0, 2)], gall.at[0, 2, cut(w, 0, 2)], south) for w in (0, 1)]
    g02n = [once(gall.at[0, 3, cut(w, 2, 2)], gall.at[0, 2, cut(w, 2, 2)], north) for w in (0, 1)]
    g11 = [once(gall.at[1, 0, cut(w, 0, 4)], gall.at[1, 1, cut(w, 0, 4)], south) for w in (0, 1)]
    g13 = [once(gall.at[1, 0, cut(w, 0, 4)], gall.at[1, 3, cut(w, 0, 4)], north) for w in (0, 1)]
    g12s = [once(gall.at[1, 1, cut(w, 0, 1)], gall.at[1, 2, cut(w, 0, 1)], south) for w in (0, 1)]
    g12x = [once(gall.at[0, 2, cut(w, 1, 2)], gall.at[1, 2, cut(w, 1, 2)], across) for w in (0, 1)]
    g12n = [once(gall.at[1, 3, cut(w, 3, 1)], gall.at[1, 2, cut(w, 3, 1)], north) for w in (0, 1)]
    at_rows = lambda w: pl.ds(w * half, half)
    qring = Ring(lambda w, h: q_ref.at[h, at_rows(w)], lambda r, w, h: qall.at[r, w * heads + h], heads)
    lring = Ring(lambda w, h: tots.at[0, w], lambda r, w, h: tots.at[r, w], 1)
    k2 = once(k_ref, kall.at[:, 2], side)
    v2 = once(v_ref, vall.at[:, 2], side)
    k1 = once(k_ref, kall.at[:, 1], twin)
    v1 = once(v_ref, vall.at[:, 1], twin)
    k3 = once(kall.at[:, 2], kall.at[:, 3], twin)
    v3 = once(vall.at[:, 2], vall.at[:, 3], twin)

    dkacc[...] = jnp.zeros_like(dkacc)
    dvacc[...] = jnp.zeros_like(dvacc)
    for w in (0, 1):
        for h in range(heads):
            qall[0, w * heads + h] = q_ref[h, w * half:(w + 1) * half]
    kall[:, 0] = k_ref[...]
    vall[:, 0] = v_ref[...]
    for r in (1, 3, 5, 7):
        @pl.when(z + r >= Z)
        def _(r=r):
            qall[r] = jnp.zeros(qall.shape[1:], BF)
            doall[r] = jnp.zeros(doall.shape[1:], BF)
            tots[r] = jnp.zeros(tots.shape[1:], F32)
            dels[r] = jnp.zeros(dels.shape[1:], F32)
    for w in (0, 1):
        tots[0, w] = jnp.zeros(tots.shape[2:], F32)
        tots[0, w, 0:heads, :] = lse_ref[:, w * half:(w + 1) * half] * LOG2E
    pl.semaphore_wait(barrier, len(peers))

    sring = Ring(lambda w, h: dels.at[0, w], lambda r, w, h: dels.at[r, w], 1)
    dring = Ring(lambda w, h: doall.at[0, w * heads + h], lambda r, w, h: doall.at[r, w * heads + h], heads)

    def hop(r, w):
        sring.hop(r, w)
        dring.hop(r, w)

    def qhop(r, w):
        lring.hop(r, w)
        qring.hop(r, w)

    def proj(a, b, w):
        at = ((xh + a) % 2 * Y + (y + b) % Y) * g_ref.shape[1]
        block = g_ref[w * half:(w + 1) * half] if a == b == 0 else gall[a, b, w * half:(w + 1) * half]
        return mm(block, w_vm[:, pl.ds(pl.multiple_of(at, 128), g_ref.shape[1])], NT)

    def project(w):
        grad = acc[w].astype(BF)
        dels[0, w] = jnp.zeros(dels.shape[2:], F32)
        for h in range(heads):
            grad_h = grad[:, h * width:(h + 1) * width]
            doall[0, w * heads + h] = grad_h
            terms = grad_h.astype(F32) * o_ref[h, w * half:(w + 1) * half].astype(F32)
            delta = jnp.sum(terms, axis=1, keepdims=True)
            dels[0, w, h:h + 1, :] = jnp.transpose(
                jnp.broadcast_to(delta, (half, 128)), (1, 0))[0:1, :]
        sring.begin(w)
        dring.begin(w)

    def line(ref, a, w, h):
        return jnp.concatenate([ref[a, w, pl.ds(h, 1), :], ref[a + 1, w, pl.ds(h, 1), :]], axis=1)

    def both(ref, a, w, h):
        i = w * heads + h
        return jnp.concatenate([ref[a, i], ref[a + 1, i]], axis=0)

    def prob_of(a, w, h):
        keys = kall[h].reshape(4 * rows, width)
        raw = mm(keys, both(qall, a, w, h), NT)
        shifted = raw * (factor * LOG2E) - line(tots, a, w, h)
        if a == 0:
            row = lax.broadcasted_iota(jnp.int32, shifted.shape, 0)
            col = lax.broadcasted_iota(jnp.int32, shifted.shape, 1)
            offs = []
            for j in range(4):
                jx, jc = j // 2, j % 2
                pj = (xb + jx) % 2 * 2 + (cb + jc) % 2
                offs.append((pj - p - j) * rows)
            off = jnp.where(
                row < 2 * rows,
                jnp.where(row < rows, offs[0], offs[1]),
                jnp.where(row < 3 * rows, offs[2], offs[3]))
            shown = (row + off <= col + w * half) | (col >= half)
            shifted = jnp.where(shown, shifted, -jnp.inf)
        return jnp.exp2(shifted)

    def front(a, w, h):
        probs[a + w, h] = prob_of(a, w, h)

    def tile(a, w, h):
        i = w * heads + h
        keys = kall[h].reshape(4 * rows, width)
        values = vall[h].reshape(4 * rows, width)
        query = both(qall, a, w, h)
        grad = both(doall, a, w, h)
        prob = probs[a + w, h] if a <= 2 else prob_of(a, w, h)
        pgrad = mm(values, grad, NT)
        score = (prob * (pgrad - line(dels, a, w, h))).astype(BF)
        dvacc[h] += mm(prob.astype(BF), grad, NN)
        dkacc[h] += mm(score, query, NN)
        part = mm(score, keys, TN)
        if a == 0:
            dq0[i] = part[:half]
        else:
            dqb[a, i] = part[:half].astype(BF)
        dqb[a + 1, i] = part[half:].astype(BF)

    def each(act):
        def one(h, carry):
            act(h)
            return carry
        lax.fori_loop(0, heads, one, 0)

    def serve(hops, h):
        if hops:
            @pl.when(h == 0)
            def _():
                for r, w in hops:
                    sring.hop(r, w)
            for r, w in hops:
                dring.step(r, w, h)

    def fronts(a, w, hops=()):
        def act(h):
            serve(hops, h)
            if a == 0:
                front(a, w, h)
            else:
                pl.when(valid(a))(lambda: front(a, w, h))
        each(act)

    def tiles(a, w, hops=(), then=None):
        def act(h):
            serve(hops, h)
            if a == 0:
                tile(a, w, h)
            else:
                pl.when(valid(a))(lambda: tile(a, w, h))
            if then is not None:
                then(h)
        each(act)

    def of(ref, r):
        return lambda w, h: ref.at[r, w * heads + h]

    r2 = Channel(of(dqb, 2), of(rbuf, 1), up, send_if=valid(2), recv_if=(z >= 1) & valid(1))
    r1 = Channel(of(sbuf, 1), of(rown, 1), up, send_if=valid(1), recv_if=z >= 1)
    r4 = Channel(of(dqb, 4), of(rbuf, 3), up, send_if=valid(4), recv_if=(z >= 1) & valid(3))
    r3 = Channel(of(sbuf, 3), of(rown, 0), plane(z + 3), send_if=valid(3), recv_if=z >= 3)
    wrapped = {
        r: Channel(
            of(dqb, r), lambda w, h: rown.at[2 + z % 5, w * heads + h], plane(z + r),
            send_if=valid(r), recv_if=z >= r)
        for r in (5, 6, 7)
    }
    t1 = Channel(lambda w, h: kv1s.at[h], lambda w, h: kv1r.at[h], twin, waves=1)
    t2 = Channel(lambda w, h: kv2s.at[h], lambda w, h: kv2r.at[h], side, waves=1)

    def merge(r, w, h, got, alone):
        i = w * heads + h

        @pl.when(got)
        def _():
            sbuf[r, i] = plus(dqb[r, i], rbuf[r, i])

        if alone is not None:
            @pl.when(alone)
            def _():
                sbuf[r, i] = dqb[r, i]

    def near(w, h):
        r2.recv(w, h)
        merge(1, w, h, z >= 1, z == 0)
        r1.start(w, h)

    def far(w, h):
        r4.recv(w, h)
        merge(3, w, h, z >= 1, z == 0)
        r3.start(w, h)

    def send2(w):
        return lambda h: r2.start(w, h)

    def send45(w):
        def then(h):
            r4.start(w, h)
            wrapped[5].start(w, h)
        return then

    def send67(w):
        def then(h):
            wrapped[6].start(w, h)
            wrapped[7].start(w, h)
        return then

    def hand_over(h):
        for j, slot in ((0, 1), (1, 3)):
            at = pl.ds(slot * rows, rows)
            kv1s[h, j, 0] = dkacc[h, at, :].astype(BF)
            kv1s[h, j, 1] = dvacc[h, at, :].astype(BF)
        t1.start(0, h)

    def fold(h):
        t1.recv(0, h)
        at = pl.ds(2 * rows, rows)
        kv2s[h, 0] = plus(dkacc[h, at, :], kv1r[h, 1, 0])
        kv2s[h, 1] = plus(dvacc[h, at, :], kv1r[h, 1, 1])
        t2.start(0, h)

    g01[0].start()
    g03[0].start()
    g10[0].start()
    lring.begin(0)
    qring.begin(0)
    g01[1].start()
    g03[1].start()
    g10[1].start()
    lring.begin(1)
    qring.begin(1)
    k2.start()
    k1.start()
    v2.start()
    v1.start()
    wcopy.wait()

    acc = [proj(0, 0, 0), proj(0, 0, 1)]
    qhop(1, 0)
    g01[0].recv()
    g02s[0].start()
    g03[0].recv()
    g02n[0].start()
    g10[0].recv()
    g11[0].start()
    g13[0].start()
    qhop(1, 1)
    acc[0] += proj(0, 1, 0)
    acc[0] += proj(0, 3, 0)
    acc[0] += proj(1, 0, 0)
    g01[1].recv()
    g02s[1].start()
    g03[1].recv()
    g02n[1].start()
    qhop(2, 0)
    g02s[0].recv()
    g02n[0].recv()
    g12x[0].start()
    qhop(2, 1)
    k1.recv()
    k2.recv()
    k3.start()
    acc[0] += proj(0, 2, 0)
    acc[1] += proj(0, 1, 1)
    acc[1] += proj(0, 3, 1)
    qhop(3, 0)
    g11[0].recv()
    g12s[0].start()
    g13[0].recv()
    g12n[0].start()
    g10[1].recv()
    g11[1].start()
    g13[1].start()
    acc[0] += proj(1, 1, 0)
    acc[0] += proj(1, 3, 0)
    acc[1] += proj(1, 0, 1)
    k3.recv()
    fronts(0, 0)
    qhop(3, 1)
    g02s[1].recv()
    g02n[1].recv()
    g12x[1].start()
    for c in (g12s[0], g12n[0], g12x[0]):
        c.recv()
    acc[0] += proj(1, 2, 0)
    project(0)
    v2.recv()
    v3.start()
    g11[1].recv()
    g12s[1].start()
    g13[1].recv()
    g12n[1].start()
    qhop(7, 0)
    qhop(7, 1)
    fronts(0, 1)
    acc[1] += proj(0, 2, 1)
    acc[1] += proj(1, 1, 1)
    acc[1] += proj(1, 3, 1)
    hop(1, 0)
    for c in (g12s[1], g12n[1], g12x[1]):
        c.recv()
    acc[1] += proj(1, 2, 1)
    project(1)
    v1.recv()
    v3.recv()
    fronts(2, 0, [(2, 0)])
    qhop(6, 0)
    qhop(6, 1)
    qhop(4, 0)
    tiles(0, 0, [(1, 1)])
    fronts(2, 1, [(3, 0)])
    tiles(2, 0, [(7, 0), (2, 1)], send2(0))
    qhop(5, 0)
    qhop(4, 1)
    tiles(0, 1, [(4, 0), (6, 0), (7, 1)])
    qhop(5, 1)
    tiles(4, 0, [(3, 1), (5, 0), (6, 1)], send45(0))
    each(lambda h: near(0, h))

    def rest(h):
        pl.when(valid(2))(lambda: tile(2, 1, h))
        send2(1)(h)
        pl.when(valid(6))(lambda: tile(6, 0, h))
        send67(0)(h)
        pl.when(valid(6))(lambda: tile(6, 1, h))
        send67(1)(h)

        @pl.when(h > 0)
        def _():
            fold(h - 1)

        serve([(4, 1), (5, 1)], h)
        pl.when(valid(4))(lambda: tile(4, 1, h))
        send45(1)(h)
        hand_over(h)
        far(0, h)

    each(rest)
    fold(heads - 1)
    each(lambda h: near(1, h))
    each(lambda h: far(1, h))

    def finish(h):
        for w in (0, 1):
            i = w * heads + h
            r1.recv(w, h)
            r3.recv(w, h)
            for r in (5, 6, 7):
                wrapped[r].recv(w, h)
            for slot, cond in ((1, z >= 1), (0, z >= 3)) + tuple((2 + z - r, z >= r) for r in (5, 6, 7)):
                @pl.when(cond)
                def _(slot=slot, i=i):
                    dq0[i] += rown[slot, i].astype(F32)
            out[0, h, at_rows(w)] = (dq0[i] * factor).astype(BF)
        t2.recv(0, h)
        at = pl.ds(0, rows)
        key_sum = dkacc[h, at, :] + kv1r[h, 0, 0].astype(F32) + kv2r[h, 0].astype(F32)
        value_sum = dvacc[h, at, :] + kv1r[h, 0, 1].astype(F32) + kv2r[h, 1].astype(F32)
        out[1, h] = (key_sum * factor).astype(BF)
        out[2, h] = value_sum.astype(BF)

    each(finish)

    for c in channels:
        c.drain()


def body(queries, key_vectors, value_vectors, attn_output, output_grad, w_out, log_total):
    rows, heads, width = queries.shape
    major = lambda a: jnp.transpose(a, (1, 0, 2))
    vmem = pl.BlockSpec(memory_space=pltpu.VMEM)
    V = pltpu.VMEM
    blk = (heads, rows, width)
    chunks = (2 * heads, rows // 2, width)
    outs = pl.pallas_call(
        kernel,
        out_shape=jax.ShapeDtypeStruct((3,) + blk, BF),
        in_specs=[vmem] * 6 + [pl.BlockSpec(memory_space=pl.ANY)],
        out_specs=vmem,
        scratch_shapes=[
            V(w_out.shape, BF),
            V((2, Y) + output_grad.shape, BF),
            V((Z,) + chunks, BF),
            V((heads, 4, rows, width), BF),
            V((heads, 4, rows, width), BF),
            V((Z,) + chunks, BF),
            V((Z, 2, 8, rows // 2), F32),
            V((Z, 2, 8, rows // 2), F32),
            V((4, heads, 4 * rows, rows), F32),
            V((Z,) + chunks, BF),
            V((Z,) + chunks, BF),
            V((Z,) + chunks, BF),
            V((5,) + chunks, BF),
            V((heads, 4 * rows, width), F32),
            V((heads, 4 * rows, width), F32),
            V(chunks, F32),
            V((heads, 2, 2, rows, width), BF),
            V((heads, 2, 2, rows, width), BF),
            V((heads, 2, rows, width), BF),
            V((heads, 2, rows, width), BF),
            pltpu.SemaphoreType.DMA,
            pltpu.SemaphoreType.DMA((COPIES,)),
            pltpu.SemaphoreType.DMA((COPIES,)),
        ],
        compiler_params=pltpu.CompilerParams(
            collective_id=0, has_side_effects=True, vmem_limit_bytes=60 * 1024 * 1024),
        name="attention_backward",
    )(
        major(queries), major(key_vectors), major(value_vectors), major(attn_output),
        output_grad, jnp.transpose(log_total, (1, 0)), w_out,
    )
    return tuple(major(outs[i]) for i in range(3))


def solution(mesh):
    row = P("ctx", "head", None)
    return jax.shard_map(
        body, mesh=mesh,
        in_specs=(row, row, row, row, P("ctx", "head"), P("head", None), P("ctx", "head")),
        out_specs=(row, row, row), check_vma=False)
```

```python
import math

import jax
import jax.numpy as jnp
from jax import lax
from jax.experimental import pallas as pl
from jax.experimental.pallas import tpu as pltpu
from jax.sharding import PartitionSpec as P

MESH = pl.DeviceIdType.MESH
BF = jnp.bfloat16
F32 = jnp.float32
LOG2E = math.log2(math.e)
Z = 8
Y = 4
COPIES = 320

NT = (((1,), (1,)), ((), ()))
TN = (((0,), (0,)), ((), ()))
NN = (((1,), (0,)), ((), ()))


def mm(a, b, dims):
    return lax.dot_general(a, b, dims, preferred_element_type=F32)


def plus(a, b):
    return (a.astype(F32) + b.astype(F32)).astype(BF)


def kernel(
    q_ref, k_ref, v_ref, o_ref, g_ref, lse_ref, w_hbm,
    out,
    w_vm, gall, qall, kall, vall, doall, tots, dels, probs, dqb, sbuf, rbuf, rown,
    dkacc, dvacc, dq0, kv1s, kv1r, kv2s, kv2r,
    w_sem, send_sem, recv_sem,
):
    heads, rows, width = q_ref.shape
    half = rows // 2
    factor = width ** -0.5
    ctx = lax.axis_index("ctx")
    hd = lax.axis_index("head")
    z = ctx // 4
    p = ctx % 4
    xb, cb = p // 2, p % 2
    xh, y = hd // Y, hd % Y

    def plane(to):
        return ((to + Z) % Z * 4 + p, hd)

    up, down = plane(z + 1), plane(z - 1)
    north = (ctx, xh * Y + (y + 1) % Y)
    south = (ctx, xh * Y + (y + Y - 1) % Y)
    across = (ctx, (1 - xh) * Y + y)
    side = (z * 4 + (1 - xb) * 2 + cb, hd)
    twin = (z * 4 + xb * 2 + 1 - cb, hd)
    peers = [plane(z + d) for d in (-3, -2, -1, 1, 2, 3)]
    peers += [north, south, across, side, twin]

    wcopy = pltpu.make_async_copy(w_hbm, w_vm, w_sem)
    wcopy.start()
    barrier = pltpu.get_barrier_semaphore()
    for peer in peers:
        pl.semaphore_signal(barrier, inc=1, device_id=peer, device_id_type=MESH)

    used = [0]
    channels = []

    def when(cond, act):
        if cond is None:
            act()
        else:
            pl.when(cond)(act)

    class Channel:
        def __init__(self, src, dst, to, send_if=None, recv_if=None, waves=2, m=heads, shift=0, slots=1):
            self.src, self.dst, self.to, self.shift = src, dst, to, shift
            self.send_if, self.recv_if, self.waves, self.m = send_if, recv_if, waves, m
            self.base = used[0]
            used[0] += waves * m * slots
            channels.append(self)

        def copy(self, w, h, shift):
            at = self.base + shift + w * self.m + h
            return pltpu.make_async_remote_copy(
                src_ref=self.src(w, h), dst_ref=self.dst(w, h),
                send_sem=send_sem.at[at], recv_sem=recv_sem.at[at],
                device_id=self.to, device_id_type=MESH)

        def start(self, w=0, h=0):
            when(self.send_if, lambda: self.copy(w, h, self.shift).start())

        def recv(self, w=0, h=0):
            when(self.recv_if, lambda: self.copy(w, h, 0).wait_recv())

        def recv_at(self, w, h, shift, cond):
            when(cond, lambda: self.copy(w, h, shift).wait_recv())

        def drain(self):
            def act():
                for w in range(self.waves):
                    for h in range(self.m):
                        self.copy(w, h, self.shift).wait_send()
            when(self.send_if, act)

    def once(src, dst, to, **kw):
        return Channel(lambda w, h: src, lambda w, h: dst, to, waves=1, m=1, **kw)

    def valid(r):
        return z + r <= Z - 1

    class Ring:
        def __init__(self, own, held, m):
            self.hops = {}
            self.m = m
            for r in range(1, 5):
                src = own if r == 1 else (lambda w, h, r=r: held(r - 1, w, h))
                self.hops[r] = Channel(
                    src, lambda w, h, r=r: held(r, w, h), down, m=m,
                    send_if=(z >= 1) & (z - 1 + r <= Z - 1), recv_if=valid(r))
            self.wrap = Channel(
                own, lambda w, h: held(z, w, h), plane(0), m=m, send_if=z >= 5,
                shift=(z - 5) * 2 * m, slots=3)
            self.seven = Channel(
                lambda w, h: held(7, w, h), lambda w, h: held(6, w, h), up, m=m,
                send_if=z == 0, recv_if=z == 1)
            self.six = Channel(
                lambda w, h: held(6, w, h), lambda w, h: held(5, w, h), up, m=m,
                send_if=z <= 1, recv_if=(z == 1) | (z == 2))

        def begin(self, w):
            for h in range(self.m):
                self.hops[1].start(w, h)
                self.wrap.start(w, h)

        def step(self, r, w, h):
            if r <= 4:
                self.hops[r].recv(w, h)
                if r < 4:
                    self.hops[r + 1].start(w, h)
            else:
                self.wrap.recv_at(w, h, (r - 5) * 2 * self.m, z == 0)
                if r == 7:
                    self.seven.start(w, h)
                if r == 6:
                    self.seven.recv(w, h)
                    self.six.start(w, h)
                if r == 5:
                    self.six.recv(w, h)

        def hop(self, r, w):
            for h in range(self.m):
                self.step(r, w, h)

    def cut(w, first, size):
        return pl.ds(w * half + first * half // 4, size * half // 4)

    g01 = [once(g_ref.at[cut(w, 0, 4)], gall.at[0, 1, cut(w, 0, 4)], south) for w in (0, 1)]
    g03 = [once(g_ref.at[cut(w, 0, 4)], gall.at[0, 3, cut(w, 0, 4)], north) for w in (0, 1)]
    g10 = [once(g_ref.at[cut(w, 0, 4)], gall.at[1, 0, cut(w, 0, 4)], across) for w in (0, 1)]
    g02s = [once(gall.at[0, 1, cut(w, 0, 2)], gall.at[0, 2, cut(w, 0, 2)], south) for w in (0, 1)]
    g02n = [once(gall.at[0, 3, cut(w, 2, 2)], gall.at[0, 2, cut(w, 2, 2)], north) for w in (0, 1)]
    g11 = [once(gall.at[1, 0, cut(w, 0, 4)], gall.at[1, 1, cut(w, 0, 4)], south) for w in (0, 1)]
    g13 = [once(gall.at[1, 0, cut(w, 0, 4)], gall.at[1, 3, cut(w, 0, 4)], north) for w in (0, 1)]
    g12s = [once(gall.at[1, 1, cut(w, 0, 1)], gall.at[1, 2, cut(w, 0, 1)], south) for w in (0, 1)]
    g12x = [once(gall.at[0, 2, cut(w, 1, 2)], gall.at[1, 2, cut(w, 1, 2)], across) for w in (0, 1)]
    g12n = [once(gall.at[1, 3, cut(w, 3, 1)], gall.at[1, 2, cut(w, 3, 1)], north) for w in (0, 1)]
    at_rows = lambda w: pl.ds(w * half, half)
    qring = Ring(lambda w, h: q_ref.at[h, at_rows(w)], lambda r, w, h: qall.at[r, w * heads + h], heads)
    lring = Ring(lambda w, h: tots.at[0, w], lambda r, w, h: tots.at[r, w], 1)
    k2 = once(k_ref, kall.at[:, 2], side)
    v2 = once(v_ref, vall.at[:, 2], side)
    k1 = once(k_ref, kall.at[:, 1], twin)
    v1 = once(v_ref, vall.at[:, 1], twin)
    k3 = once(kall.at[:, 2], kall.at[:, 3], twin)
    v3 = once(vall.at[:, 2], vall.at[:, 3], twin)

    dkacc[...] = jnp.zeros_like(dkacc)
    dvacc[...] = jnp.zeros_like(dvacc)
    for w in (0, 1):
        for h in range(heads):
            qall[0, w * heads + h] = q_ref[h, w * half:(w + 1) * half]
    kall[:, 0] = k_ref[...]
    vall[:, 0] = v_ref[...]
    for r in (1, 3, 5, 7):
        @pl.when(z + r >= Z)
        def _(r=r):
            qall[r] = jnp.zeros(qall.shape[1:], BF)
            doall[r] = jnp.zeros(doall.shape[1:], BF)
            tots[r] = jnp.zeros(tots.shape[1:], F32)
            dels[r] = jnp.zeros(dels.shape[1:], F32)
    for w in (0, 1):
        tots[0, w] = jnp.zeros(tots.shape[2:], F32)
        tots[0, w, 0:heads, :] = lse_ref[:, w * half:(w + 1) * half] * LOG2E
    pl.semaphore_wait(barrier, len(peers))

    sring = Ring(lambda w, h: dels.at[0, w], lambda r, w, h: dels.at[r, w], 1)
    dring = Ring(lambda w, h: doall.at[0, w * heads + h], lambda r, w, h: doall.at[r, w * heads + h], heads)

    def hop(r, w):
        sring.hop(r, w)
        dring.hop(r, w)

    def qhop(r, w):
        lring.hop(r, w)
        qring.hop(r, w)

    def proj(a, b, w):
        at = ((xh + a) % 2 * Y + (y + b) % Y) * g_ref.shape[1]
        block = g_ref[w * half:(w + 1) * half] if a == b == 0 else gall[a, b, w * half:(w + 1) * half]
        return mm(block, w_vm[:, pl.ds(pl.multiple_of(at, 128), g_ref.shape[1])], NT)

    def project(w):
        grad = acc[w].astype(BF)
        dels[0, w] = jnp.zeros(dels.shape[2:], F32)
        for h in range(heads):
            grad_h = grad[:, h * width:(h + 1) * width]
            doall[0, w * heads + h] = grad_h
            terms = grad_h.astype(F32) * o_ref[h, w * half:(w + 1) * half].astype(F32)
            delta = jnp.sum(terms, axis=1, keepdims=True)
            dels[0, w, h:h + 1, :] = jnp.transpose(
                jnp.broadcast_to(delta, (half, 128)), (1, 0))[0:1, :]
        sring.begin(w)
        dring.begin(w)

    def line(ref, a, w, h):
        return jnp.concatenate([ref[a, w, pl.ds(h, 1), :], ref[a + 1, w, pl.ds(h, 1), :]], axis=1)

    def both(ref, a, w, h):
        i = w * heads + h
        return jnp.concatenate([ref[a, i], ref[a + 1, i]], axis=0)

    def prob_of(a, w, h):
        keys = kall[h].reshape(4 * rows, width)
        raw = mm(keys, both(qall, a, w, h), NT)
        shifted = raw * (factor * LOG2E) - line(tots, a, w, h)
        if a == 0:
            row = lax.broadcasted_iota(jnp.int32, shifted.shape, 0)
            col = lax.broadcasted_iota(jnp.int32, shifted.shape, 1)
            offs = []
            for j in range(4):
                jx, jc = j // 2, j % 2
                pj = (xb + jx) % 2 * 2 + (cb + jc) % 2
                offs.append((pj - p - j) * rows)
            off = jnp.where(
                row < 2 * rows,
                jnp.where(row < rows, offs[0], offs[1]),
                jnp.where(row < 3 * rows, offs[2], offs[3]))
            shown = (row + off <= col + w * half) | (col >= half)
            shifted = jnp.where(shown, shifted, -jnp.inf)
        return jnp.exp2(shifted)

    def front(a, w, h):
        probs[a + w, h] = prob_of(a, w, h)

    def tile(a, w, h):
        i = w * heads + h
        keys = kall[h].reshape(4 * rows, width)
        values = vall[h].reshape(4 * rows, width)
        query = both(qall, a, w, h)
        grad = both(doall, a, w, h)
        prob = probs[a + w, h] if a <= 2 else prob_of(a, w, h)
        pgrad = mm(values, grad, NT)
        score = (prob * (pgrad - line(dels, a, w, h))).astype(BF)
        dvacc[h] += mm(prob.astype(BF), grad, NN)
        dkacc[h] += mm(score, query, NN)
        part = mm(score, keys, TN)
        if a == 0:
            dq0[i] = part[:half]
        else:
            dqb[a, i] = part[:half].astype(BF)
        dqb[a + 1, i] = part[half:].astype(BF)

    def each(act):
        def one(h, carry):
            act(h)
            return carry
        lax.fori_loop(0, heads, one, 0)

    def serve(hops, h):
        if hops:
            @pl.when(h == 0)
            def _():
                for r, w in hops:
                    sring.hop(r, w)
            for r, w in hops:
                dring.step(r, w, h)

    def fronts(a, w, hops=()):
        def act(h):
            serve(hops, h)
            if a == 0:
                front(a, w, h)
            else:
                pl.when(valid(a))(lambda: front(a, w, h))
        each(act)

    def tiles(a, w, hops=(), then=None):
        def act(h):
            serve(hops, h)
            if a == 0:
                tile(a, w, h)
            else:
                pl.when(valid(a))(lambda: tile(a, w, h))
            if then is not None:
                then(h)
        each(act)

    def of(ref, r):
        return lambda w, h: ref.at[r, w * heads + h]

    r2 = Channel(of(dqb, 2), of(rbuf, 1), up, send_if=valid(2), recv_if=(z >= 1) & valid(1))
    r1 = Channel(of(sbuf, 1), of(rown, 1), up, send_if=valid(1), recv_if=z >= 1)
    r4 = Channel(of(dqb, 4), of(rbuf, 3), up, send_if=valid(4), recv_if=(z >= 1) & valid(3))
    r3 = Channel(of(sbuf, 3), of(rown, 0), plane(z + 3), send_if=valid(3), recv_if=z >= 3)
    wrapped = {
        r: Channel(
            of(dqb, r), lambda w, h: rown.at[2 + z % 5, w * heads + h], plane(z + r),
            send_if=valid(r), recv_if=z >= r)
        for r in (5, 6, 7)
    }
    t1 = Channel(lambda w, h: kv1s.at[h], lambda w, h: kv1r.at[h], twin, waves=1)
    t2 = Channel(lambda w, h: kv2s.at[h], lambda w, h: kv2r.at[h], side, waves=1)

    def merge(r, w, h, got, alone):
        i = w * heads + h

        @pl.when(got)
        def _():
            sbuf[r, i] = plus(dqb[r, i], rbuf[r, i])

        if alone is not None:
            @pl.when(alone)
            def _():
                sbuf[r, i] = dqb[r, i]

    def near(w, h):
        r2.recv(w, h)
        merge(1, w, h, z >= 1, z == 0)
        r1.start(w, h)

    def far(w, h):
        r4.recv(w, h)
        merge(3, w, h, z >= 1, z == 0)
        r3.start(w, h)

    def send2(w):
        return lambda h: r2.start(w, h)

    def send45(w):
        def then(h):
            r4.start(w, h)
            wrapped[5].start(w, h)
        return then

    def send67(w):
        def then(h):
            wrapped[6].start(w, h)
            wrapped[7].start(w, h)
        return then

    def hand_over(h):
        for j, slot in ((0, 1), (1, 3)):
            at = pl.ds(slot * rows, rows)
            kv1s[h, j, 0] = dkacc[h, at, :].astype(BF)
            kv1s[h, j, 1] = dvacc[h, at, :].astype(BF)
        t1.start(0, h)

    def fold(h):
        t1.recv(0, h)
        at = pl.ds(2 * rows, rows)
        kv2s[h, 0] = plus(dkacc[h, at, :], kv1r[h, 1, 0])
        kv2s[h, 1] = plus(dvacc[h, at, :], kv1r[h, 1, 1])
        t2.start(0, h)

    g01[0].start()
    g03[0].start()
    g10[0].start()
    lring.begin(0)
    qring.begin(0)
    g01[1].start()
    g03[1].start()
    g10[1].start()
    lring.begin(1)
    qring.begin(1)
    k2.start()
    k1.start()
    v2.start()
    v1.start()
    wcopy.wait()

    acc = [proj(0, 0, 0), proj(0, 0, 1)]
    qhop(1, 0)
    g01[0].recv()
    g02s[0].start()
    g03[0].recv()
    g02n[0].start()
    g10[0].recv()
    g11[0].start()
    g13[0].start()
    qhop(1, 1)
    acc[0] += proj(0, 1, 0)
    acc[0] += proj(0, 3, 0)
    acc[0] += proj(1, 0, 0)
    g01[1].recv()
    g02s[1].start()
    g03[1].recv()
    g02n[1].start()
    qhop(2, 0)
    g02s[0].recv()
    g02n[0].recv()
    g12x[0].start()
    qhop(2, 1)
    k1.recv()
    k2.recv()
    k3.start()
    acc[0] += proj(0, 2, 0)
    acc[1] += proj(0, 1, 1)
    acc[1] += proj(0, 3, 1)
    qhop(3, 0)
    g11[0].recv()
    g12s[0].start()
    g13[0].recv()
    g12n[0].start()
    g10[1].recv()
    g11[1].start()
    g13[1].start()
    acc[0] += proj(1, 1, 0)
    acc[0] += proj(1, 3, 0)
    acc[1] += proj(1, 0, 1)
    k3.recv()
    fronts(0, 0)
    qhop(3, 1)
    g02s[1].recv()
    g02n[1].recv()
    g12x[1].start()
    for c in (g12s[0], g12n[0], g12x[0]):
        c.recv()
    acc[0] += proj(1, 2, 0)
    project(0)
    v2.recv()
    v3.start()
    g11[1].recv()
    g12s[1].start()
    g13[1].recv()
    g12n[1].start()
    qhop(7, 0)
    qhop(7, 1)
    fronts(0, 1)
    acc[1] += proj(0, 2, 1)
    acc[1] += proj(1, 1, 1)
    acc[1] += proj(1, 3, 1)
    hop(1, 0)
    for c in (g12s[1], g12n[1], g12x[1]):
        c.recv()
    acc[1] += proj(1, 2, 1)
    project(1)
    v1.recv()
    v3.recv()
    fronts(2, 0, [(2, 0)])
    qhop(6, 0)
    qhop(6, 1)
    qhop(4, 0)
    tiles(0, 0, [(1, 1)])
    fronts(2, 1, [(3, 0)])
    tiles(2, 0, [(7, 0), (2, 1)], send2(0))
    qhop(5, 0)
    qhop(4, 1)
    tiles(0, 1, [(4, 0), (6, 0), (7, 1)])
    qhop(5, 1)
    tiles(4, 0, [(3, 1), (5, 0), (6, 1)], send45(0))
    each(lambda h: near(0, h))

    def rest(h):
        pl.when(valid(2))(lambda: tile(2, 1, h))
        send2(1)(h)
        pl.when(valid(6))(lambda: tile(6, 0, h))
        send67(0)(h)
        pl.when(valid(6))(lambda: tile(6, 1, h))
        send67(1)(h)

        @pl.when(h > 0)
        def _():
            fold(h - 1)

        serve([(4, 1), (5, 1)], h)
        pl.when(valid(4))(lambda: tile(4, 1, h))
        send45(1)(h)
        hand_over(h)
        far(0, h)

    each(rest)
    fold(heads - 1)

    def returns(h):
        near(1, h)
        far(1, h)

    each(returns)

    def finish(h):
        for w in (0, 1):
            i = w * heads + h
            r1.recv(w, h)
            r3.recv(w, h)
            for r in (5, 6, 7):
                wrapped[r].recv(w, h)
            for slot, cond in ((1, z >= 1), (0, z >= 3)) + tuple((2 + z - r, z >= r) for r in (5, 6, 7)):
                @pl.when(cond)
                def _(slot=slot, i=i):
                    dq0[i] += rown[slot, i].astype(F32)
            out[0, h, at_rows(w)] = (dq0[i] * factor).astype(BF)
        t2.recv(0, h)
        at = pl.ds(0, rows)
        key_sum = dkacc[h, at, :] + kv1r[h, 0, 0].astype(F32) + kv2r[h, 0].astype(F32)
        value_sum = dvacc[h, at, :] + kv1r[h, 0, 1].astype(F32) + kv2r[h, 1].astype(F32)
        out[1, h] = (key_sum * factor).astype(BF)
        out[2, h] = value_sum.astype(BF)

    each(finish)

    for c in channels:
        c.drain()


def body(queries, key_vectors, value_vectors, attn_output, output_grad, w_out, log_total):
    rows, heads, width = queries.shape
    major = lambda a: jnp.transpose(a, (1, 0, 2))
    vmem = pl.BlockSpec(memory_space=pltpu.VMEM)
    V = pltpu.VMEM
    blk = (heads, rows, width)
    chunks = (2 * heads, rows // 2, width)
    outs = pl.pallas_call(
        kernel,
        out_shape=jax.ShapeDtypeStruct((3,) + blk, BF),
        in_specs=[vmem] * 6 + [pl.BlockSpec(memory_space=pl.ANY)],
        out_specs=vmem,
        scratch_shapes=[
            V(w_out.shape, BF),
            V((2, Y) + output_grad.shape, BF),
            V((Z,) + chunks, BF),
            V((heads, 4, rows, width), BF),
            V((heads, 4, rows, width), BF),
            V((Z,) + chunks, BF),
            V((Z, 2, 8, rows // 2), F32),
            V((Z, 2, 8, rows // 2), F32),
            V((4, heads, 4 * rows, rows), F32),
            V((Z,) + chunks, BF),
            V((Z,) + chunks, BF),
            V((Z,) + chunks, BF),
            V((5,) + chunks, BF),
            V((heads, 4 * rows, width), F32),
            V((heads, 4 * rows, width), F32),
            V(chunks, F32),
            V((heads, 2, 2, rows, width), BF),
            V((heads, 2, 2, rows, width), BF),
            V((heads, 2, rows, width), BF),
            V((heads, 2, rows, width), BF),
            pltpu.SemaphoreType.DMA,
            pltpu.SemaphoreType.DMA((COPIES,)),
            pltpu.SemaphoreType.DMA((COPIES,)),
        ],
        compiler_params=pltpu.CompilerParams(
            collective_id=0, has_side_effects=True, vmem_limit_bytes=60 * 1024 * 1024),
        name="attention_backward",
    )(
        major(queries), major(key_vectors), major(value_vectors), major(attn_output),
        output_grad, jnp.transpose(log_total, (1, 0)), w_out,
    )
    return tuple(major(outs[i]) for i in range(3))


def solution(mesh):
    row = P("ctx", "head", None)
    return jax.shard_map(
        body, mesh=mesh,
        in_specs=(row, row, row, row, P("ctx", "head"), P("head", None), P("ctx", "head")),
        out_specs=(row, row, row), check_vma=False)
```
